32 devices in a mesh: wide: 16 (over z, x, core), narrow: 2 (over y).
Axes of the slice: x: 2, y: 2, z: 4, core: 2. Of those that a mesh axis runs over, the one named last changes fastest.
Arguments:
- query_rows: bfloat16 [640, 6144], P('wide', 'narrow'), may hold values from -30 to 30
- key_rows: bfloat16 [640, 6144], P('wide', 'narrow'), may hold values from -10 to 10
- value_rows: bfloat16 [640, 6144], P('wide', 'narrow'), may hold values from -6 to 6
- mid_grad: bfloat16 [5120, 2048], P(('wide', 'narrow')), may hold values from -6 to 6
- link_weight: bfloat16 [768, 2048], replicated, may hold values from -0.21875 to 0.21875
Outputs:
- query_grad: bfloat16 [640, 6144], P('wide', 'narrow')
- key_grad: bfloat16 [640, 6144], P('wide', 'narrow')
- value_grad: bfloat16 [640, 6144], P('wide', 'narrow')
The draws below stay inside these ranges and needn't reach their ends.
All inputs are finite; a program needn't handle non-finite values.
Results may differ from the reference program's by a relative error of at most 0.0066.
Values may be sent and summed in bfloat16 or wider, within the bound.
No kernel may reach another device: no remote copies, remote signals or barrier semaphores. Data moves between devices by JAX's collectives and lax.ppermute only.
A program may use at most 64 MiB of HBM per device.

```python
import math
import jax
import jax.numpy as jnp
from jax import lax

DG = 6144
HD = 128
HEADS = 48
DM = 2048
PATCH = 8
DP = 768
TP = 640


def joint_rows(key):
    key_query, key_keys = jax.random.split(key, 2)
    shape = (TP, DG)
    queries = jnp.clip(jax.random.normal(key_query, shape, jnp.float32), -6.0, 6.0)
    keys_drawn = jnp.clip(jax.random.normal(key_keys, shape, jnp.float32), -6.0, 6.0)
    return (queries, keys_drawn)


def draw_query_rows(key, part):
    queries, keys_drawn = joint_rows(jax.random.fold_in(key, 7))
    return queries.astype(jnp.bfloat16)


def draw_key_rows(key, part):
    queries, keys_drawn = joint_rows(jax.random.fold_in(key, 7))
    return keys_drawn.astype(jnp.bfloat16)


def levels(key, extent, cuts, low, top_value):
    factor_of = 1.0
    for dim, blocks in cuts:
        steps = jax.random.uniform(jax.random.fold_in(jax.random.fold_in(key, 6), dim), (blocks,), jnp.float32, low / len(cuts), top_value / len(cuts))
        factor_of = factor_of * jnp.repeat(jnp.exp(steps), extent[dim] // blocks).reshape((-1,) + (1,) * (len(extent) - 1 - dim))
    return factor_of


def gaussian(stream_key, dims, scale, bound, cuts=(), kind=jnp.bfloat16):
    drawn = scale * jax.random.normal(stream_key, dims, jnp.float32)
    if cuts:
        drawn = drawn * levels(stream_key, dims, cuts, -0.22, 0.18)
    return jnp.clip(drawn, -bound, bound).astype(kind)


def setup_inputs(seed: int = 0) -> dict:
    arg_keys = jax.random.split(jax.random.key(seed), 6)
    query_rows = draw_query_rows(jax.random.fold_in(arg_keys[5], 71), 0)
    key_rows = draw_key_rows(jax.random.fold_in(arg_keys[5], 71), 0)
    value_rows = gaussian(arg_keys[2], (TP, DG), 1.0, 6.0, ((0, 16), (1, 2)))
    mid_grad = gaussian(arg_keys[3], (TP * PATCH, DM), 1.0, 6.0, ((0, 32),))
    link_weight = gaussian(arg_keys[4], (DP, DM), DP ** -0.5, 0.21875)
    return dict(query_rows=query_rows, key_rows=key_rows, value_rows=value_rows, mid_grad=mid_grad, link_weight=link_weight)


def head_grads(parts):
    query_head, key_head, value_head, grad_head = parts
    length = query_head.shape[0]
    scaling = 1.0 / math.sqrt(HD)
    scores = jnp.dot(query_head, key_head.T, preferred_element_type=jnp.float32) * scaling
    allowed = jnp.tril(jnp.ones((length, length), dtype=jnp.bool_))
    scores = jnp.where(allowed, scores, -jnp.inf)
    biggest = lax.optimization_barrier(jnp.max(scores, axis=1, keepdims=True))
    log_total = biggest + jnp.log(lax.optimization_barrier(jnp.sum(jnp.exp(scores - biggest), axis=1, keepdims=True)))
    products = jnp.dot(grad_head, value_head.T, preferred_element_type=jnp.float32)
    weights = jnp.where(allowed, jnp.exp(scores - log_total), 0.0)
    row_delta = lax.optimization_barrier(jnp.sum(weights * products, axis=1, keepdims=True))
    score_grad = (weights * (products - row_delta)).astype(jnp.bfloat16)
    query_part = (jnp.dot(score_grad, key_head, preferred_element_type=jnp.float32) * scaling).astype(jnp.bfloat16)
    key_part = (jnp.dot(score_grad.T, query_head, preferred_element_type=jnp.float32) * scaling).astype(jnp.bfloat16)
    value_part = jnp.dot(weights.astype(jnp.bfloat16).T, grad_head, preferred_element_type=jnp.float32).astype(jnp.bfloat16)
    return (query_part, key_part, value_part)

def reference(query_rows, key_rows, value_rows, mid_grad, link_weight):
    length = query_rows.shape[0]
    incoming = jnp.dot(mid_grad, link_weight.T, preferred_element_type=jnp.float32).astype(jnp.bfloat16)
    incoming = incoming.reshape(length, DG)

    def by_head(matrix):
        return matrix.reshape(length, HEADS, HD).transpose(1, 0, 2)

    def back(stacked):
        return stacked.transpose(1, 0, 2).reshape(length, DG)
    query_part, key_part, value_part = lax.map(head_grads, (by_head(query_rows), by_head(key_rows), by_head(value_rows), by_head(incoming)))
    return (back(query_part), back(key_part), back(value_part))
```

```python
import math

import jax
import jax.numpy as jnp
from jax import lax
from jax.experimental import pallas as pl
from jax.experimental.pallas import tpu as pltpu
from jax.sharding import PartitionSpec as P

HD = 128
PATCH = 8
TILE = 128


lowest = -1e30


def grid_spec(blocks, outs, scratch=()):
    vmem = pl.BlockSpec(memory_space=pltpu.VMEM)
    return pltpu.PrefetchScalarGridSpec(
        num_scalar_prefetch=1,
        grid=(1,),
        in_specs=[vmem] * blocks,
        out_specs=[vmem] * outs,
        scratch_shapes=list(scratch),
    )


def pack(place, arrays, chips):
    rows, columns = arrays[0].shape
    wide = columns // chips

    def kernel(place_ref, *refs):
        ins, outs = refs[: len(arrays)], refs[len(arrays) :]
        for step in range(chips):
            start = pl.multiple_of((place_ref[0] ^ step) * wide, HD)
            for which, ref in enumerate(ins):
                outs[step][:, which * wide : (which + 1) * wide] = ref[:, pl.ds(start, wide)]

    shape = jax.ShapeDtypeStruct((rows, len(arrays) * wide), arrays[0].dtype)
    return pl.pallas_call(
        kernel,
        grid_spec=grid_spec(len(arrays), chips),
        out_shape=[shape] * chips,
        cost_estimate=pl.CostEstimate(
            flops=0, bytes_accessed=4 * len(arrays) * rows * columns, transcendentals=0
        ),
        name="pack",
    )(place, *arrays)


def attend(place, own, other, rows):
    chips = len(own)
    total = 2 * chips * rows
    scaling = 1.0 / math.sqrt(HD)
    tiles = total // TILE

    def kernel(place_ref, *refs):
        own_refs, other_refs = refs[:chips], refs[chips : 2 * chips]
        outs = refs[2 * chips : 3 * chips]
        gathered, query_sum, key_sum, value_sum = refs[3 * chips :]
        chip, core = place_ref[0], place_ref[1]

        def spots(step):
            start = (chip ^ step) * (2 * rows)
            return (
                pl.ds(pl.multiple_of(start + core * rows, 8), rows),
                pl.ds(pl.multiple_of(start + (1 - core) * rows, 8), rows),
            )

        for index in range(2):
            head = core + index
            for which in range(4):
                lanes = pl.ds(pl.multiple_of((which * 3 + head) * HD, HD), HD)
                for step in range(chips):
                    mine, others = spots(step)
                    gathered[which, mine, :] = own_refs[step][:, lanes].astype(jnp.float32)
                    gathered[which, others, :] = other_refs[step][:, lanes].astype(jnp.float32)
            query = gathered[0].astype(jnp.bfloat16)
            keys = gathered[1].astype(jnp.bfloat16)
            values = gathered[2].astype(jnp.bfloat16)
            grads = gathered[3].astype(jnp.bfloat16)
            for tile in range(tiles):
                low, high = tile * TILE, (tile + 1) * TILE
                q, g = query[low:high], grads[low:high]
                k, v = keys[:high], values[:high]
                last = (((1,), (1,)), ((), ()))
                first = (((0,), (0,)), ((), ()))
                scores = scaling * lax.dot_general(q, k, last, preferred_element_type=jnp.float32)
                row = lax.broadcasted_iota(jnp.int32, (TILE, high), 0) + low
                col = lax.broadcasted_iota(jnp.int32, (TILE, high), 1)
                scores = jnp.where(col <= row, scores, lowest)
                expo = jnp.exp(scores - jnp.max(scores, axis=1, keepdims=True))
                products = lax.dot_general(g, v, last, preferred_element_type=jnp.float32)
                scale = 1.0 / jnp.sum(expo, axis=1, keepdims=True)
                delta = jnp.sum(expo * products, axis=1, keepdims=True) * scale
                weights = expo * scale
                score_grad = (weights * (products - delta)).astype(jnp.bfloat16)
                half = weights.astype(jnp.bfloat16)
                query_sum[low:high] = lax.dot_general(
                    score_grad, k, (((1,), (0,)), ((), ())), preferred_element_type=jnp.float32
                )
                key_part = lax.dot_general(score_grad, q, first, preferred_element_type=jnp.float32)
                value_part = lax.dot_general(half, g, first, preferred_element_type=jnp.float32)
                if tile:
                    key_sum[:low] += key_part[:low]
                    value_sum[:low] += value_part[:low]
                key_sum[low:high] = key_part[low:]
                value_sum[low:high] = value_part[low:]
            shared = head == 1
            for which, (store, factor) in enumerate(
                ((query_sum, scaling), (key_sum, scaling), (value_sum, None))
            ):
                lanes = slice(which * HD, (which + 1) * HD)
                for step in range(chips):
                    mine, others = spots(step)

                    def rounded(spot):
                        block = store[spot]
                        return (block if factor is None else block * factor).astype(jnp.bfloat16)

                    @pl.when(shared)
                    def _():
                        outs[step][1, :, lanes] = rounded(mine)

                    @pl.when(jnp.logical_not(shared))
                    def _():
                        outs[step][0, :, lanes] = rounded(mine)
                        outs[step][2, :, lanes] = rounded(others)

    shape = jax.ShapeDtypeStruct((3, rows, 3 * HD), own[0].dtype)
    big = pltpu.VMEM((total, HD), jnp.float32)
    return pl.pallas_call(
        kernel,
        grid_spec=grid_spec(
            2 * chips, chips, (pltpu.VMEM((4, total, HD), jnp.float32), big, big, big)
        ),
        out_shape=[shape] * chips,
        cost_estimate=pl.CostEstimate(
            flops=10 * total * total * HD,
            bytes_accessed=22 * total * 3 * HD,
            transcendentals=2 * total * total,
        ),
        name="attend",
    )(place, *own, *other)


def unpack(place, own, other, rows, columns):
    chips = len(own)
    wide = columns // chips

    def kernel(place_ref, *refs):
        own_refs, other_refs, outs = refs[:chips], refs[chips : 2 * chips], refs[2 * chips :]
        core = place_ref[1]
        for step in range(chips):
            start = (place_ref[0] ^ step) * wide
            for which, out in enumerate(outs):
                lanes = slice(which * HD, (which + 1) * HD)

                def put(head, block):
                    out[:, pl.ds(pl.multiple_of(start + head * HD, HD), HD)] = block

                put(2 * core, own_refs[step][0, :, lanes])
                put(1, own_refs[step][1, :, lanes])
                put(2 - 2 * core, other_refs[step][2, :, lanes])

    shape = jax.ShapeDtypeStruct((rows, columns), own[0].dtype)
    return pl.pallas_call(
        kernel,
        grid_spec=grid_spec(2 * chips, 3),
        out_shape=[shape] * 3,
        cost_estimate=pl.CostEstimate(
            flops=0, bytes_accessed=16 * rows * columns, transcendentals=0
        ),
        name="unpack",
    )(place, *own, *other)


def by_heads(query_rows, key_rows, value_rows, mid_grad, link_weight):
    rows, columns = query_rows.shape
    size = lax.axis_size("wide")
    chips = size // 2
    me, side = lax.axis_index("wide"), lax.axis_index("narrow")
    place = jnp.stack([me // 2, me % 2]).astype(jnp.int32)

    flat = lax.dot_general(
        mid_grad, link_weight, (((1,), (1,)), ((), ())), preferred_element_type=jnp.float32
    ).astype(jnp.bfloat16)
    flat = flat.reshape(rows // 2, 2 * columns)
    stay = lax.dynamic_slice_in_dim(flat, side * columns, columns, axis=1)
    leave = lax.dynamic_slice_in_dim(flat, (1 - side) * columns, columns, axis=1)
    came = lax.ppermute(leave, "narrow", [(0, 1), (1, 0)])
    incoming = jnp.where(
        side == 0, jnp.concatenate([stay, came]), jnp.concatenate([came, stay])
    )

    def cross(block, step):
        return lax.ppermute(block, "wide", [(i, i ^ step) for i in range(size)])

    sent = pack(place, [query_rows, key_rows, value_rows, incoming], chips)
    own = [sent[0]] + [cross(sent[step], 2 * step) for step in range(1, chips)]
    other = [cross(block, 1) for block in own]
    done = attend(place, own, other, rows)
    own = [done[0]] + [cross(done[step], 2 * step) for step in range(1, chips)]
    other = [cross(block, 1) for block in own]
    return tuple(unpack(place, own, other, rows, columns))


def on_device(query_rows, key_rows, value_rows, mid_grad, link_weight):
    size = lax.axis_size("wide")
    rows, columns = query_rows.shape
    chips = size // 2
    fits = (
        size > 1
        and size & (size - 1) == 0
        and lax.axis_size("narrow") == 2
        and columns == chips * 3 * HD
        and (size * rows) % TILE == 0
        and rows % 8 == 0
    )
    plan = by_heads if fits else by_rows
    return plan(query_rows, key_rows, value_rows, mid_grad, link_weight)


def by_rows(query_rows, key_rows, value_rows, mid_grad, link_weight):
    groups = lax.axis_size("narrow")
    patches = query_rows.shape[0]
    columns = query_rows.shape[1]
    heads_here = columns // HD
    scaling = 1.0 / math.sqrt(HD)
    local_patches = mid_grad.shape[0] // PATCH
    grouped = mid_grad.reshape(local_patches, groups, PATCH // groups, mid_grad.shape[1])
    moved = jnp.einsum(
        "abcm,pm->abcp",
        lax.all_to_all(grouped, "narrow", split_axis=1, concat_axis=0, tiled=True),
        link_weight,
        preferred_element_type=jnp.float32,
    ).astype(jnp.bfloat16)
    incoming = moved.reshape(patches, columns)
    incoming_heads = incoming.reshape(patches, heads_here, HD)
    query_heads = query_rows.reshape(patches, heads_here, HD)
    key_heads = key_rows.reshape(patches, heads_here, HD)
    value_heads = value_rows.reshape(patches, heads_here, HD)
    own_pos = lax.axis_index("wide") * patches + jnp.arange(patches, dtype=jnp.int32)
    total_rows = patches * lax.axis_size("wide")
    empty_store = jnp.zeros((total_rows, columns), jnp.bfloat16)
    fold_start = (
        jnp.full((heads_here, patches), lowest, jnp.float32),
        jnp.zeros((heads_here, patches), jnp.float32),
        jnp.zeros((heads_here, patches), jnp.float32),
        empty_store,
        empty_store,
    )
    pieces = (
        lax.all_gather(key_rows, "wide", axis=0, tiled=True),
        lax.all_gather(value_rows, "wide", axis=0, tiled=True),
    )
    key_piece, value_piece = pieces
    piece_rows = key_piece.shape[0]
    key_split = key_piece.reshape(piece_rows, heads_here, HD)
    value_split = value_piece.reshape(piece_rows, heads_here, HD)
    piece_pos = jnp.arange(piece_rows, dtype=jnp.int32)
    allowed = piece_pos[None, None, :] <= own_pos[None, :, None]
    scores = (
        jnp.einsum("qhd,khd->hqk", query_heads, key_split, preferred_element_type=jnp.float32)
        * scaling
    )
    scores = jnp.where(allowed, scores, lowest)
    products = jnp.einsum(
        "qhd,khd->hqk", incoming_heads, value_split, preferred_element_type=jnp.float32
    )
    old_max, old_total, old_tilt = fold_start[:3]
    new_max = jnp.maximum(old_max, jnp.max(scores, axis=2))
    expo = jnp.where(allowed, jnp.exp(scores - new_max[:, :, None]), 0.0)
    stats = (new_max, jnp.sum(expo, axis=2), jnp.sum(expo * products, axis=2))
    key_store = pieces[0]
    value_store = pieces[1]
    folded = stats + (key_store, value_store)
    run_max, run_total, run_tilt = (folded[0], folded[1], folded[2])
    log_total = run_max + jnp.log(run_total)
    row_delta = run_tilt / run_total
    key_all = folded[3].reshape(total_rows, heads_here, HD)
    value_all = folded[4].reshape(total_rows, heads_here, HD)
    every_pos = jnp.arange(total_rows, dtype=jnp.int32)
    allowed_q = every_pos[None, None, :] <= own_pos[None, :, None]
    scores_q = (
        jnp.einsum("qhd,khd->hqk", query_heads, key_all, preferred_element_type=jnp.float32)
        * scaling
    )
    products_q = jnp.einsum(
        "qhd,khd->hqk", incoming_heads, value_all, preferred_element_type=jnp.float32
    )
    weights_q = jnp.where(
        allowed_q, jnp.exp(jnp.where(allowed_q, scores_q, lowest) - log_total[:, :, None]), 0.0
    )
    score_grad_q = (weights_q * (products_q - row_delta[:, :, None])).astype(jnp.bfloat16)
    query_accum = jnp.einsum(
        "hqk,khd->qhd", score_grad_q, key_all, preferred_element_type=jnp.float32
    )
    query_grad = (query_accum * scaling).astype(jnp.bfloat16).reshape(patches, columns)
    total_all, delta_all = (
        lax.all_gather(log_total, "wide", axis=1, tiled=True),
        lax.all_gather(row_delta, "wide", axis=1, tiled=True),
    )
    query_piece = lax.all_gather(query_rows, "wide", axis=0, tiled=True)
    grad_piece = lax.all_gather(incoming, "wide", axis=0, tiled=True)
    piece_rows = query_piece.shape[0]
    query_split = query_piece.reshape(piece_rows, heads_here, HD)
    grad_split = grad_piece.reshape(piece_rows, heads_here, HD)
    piece_pos = jnp.arange(piece_rows, dtype=jnp.int32)
    allowed = own_pos[None, None, :] <= piece_pos[None, :, None]
    scores = (
        jnp.einsum("qhd,khd->hqk", query_split, key_heads, preferred_element_type=jnp.float32)
        * scaling
    )
    scores = jnp.where(allowed, scores, lowest)
    products = jnp.einsum(
        "qhd,khd->hqk", grad_split, value_heads, preferred_element_type=jnp.float32
    )
    weights = jnp.where(allowed, jnp.exp(scores - total_all[:, :, None]), 0.0)
    score_grad = (weights * (products - delta_all[:, :, None])).astype(jnp.bfloat16)
    key_accum = jnp.einsum(
        "hqk,qhd->khd", score_grad, query_split, preferred_element_type=jnp.float32
    )
    value_accum = jnp.einsum(
        "hqk,qhd->khd", weights.astype(jnp.bfloat16), grad_split, preferred_element_type=jnp.float32
    )
    key_accum, value_accum = (key_accum, value_accum)
    key_grad = (key_accum * scaling).astype(jnp.bfloat16).reshape(patches, columns)
    value_grad = value_accum.astype(jnp.bfloat16).reshape(patches, columns)
    return (query_grad, key_grad, value_grad)


def solution(mesh):
    in_specs = (
        P("wide", "narrow"),
        P("wide", "narrow"),
        P("wide", "narrow"),
        P(("wide", "narrow"), None),
        P(),
    )
    out_specs = (P("wide", "narrow"), P("wide", "narrow"), P("wide", "narrow"))
    return jax.shard_map(
        on_device, mesh=mesh, in_specs=in_specs, out_specs=out_specs, check_vma=False
    )
```

```python
import math

import jax
import jax.numpy as jnp
from jax import lax
from jax.experimental import pallas as pl
from jax.experimental.pallas import tpu as pltpu
from jax.sharding import PartitionSpec as P


HD = 128
PATCH = 8
TILE = 128
ROOM = 24 << 20


lowest = -1e30


def in_order(chips):
    far = list(range(chips // 2, chips))
    near = list(range(1, chips // 2))[::-1]
    return far[:2], far[2:] + near


def local(kernel, ins, shapes, scratch=(), flops=0, final=False):
    vmem = pl.BlockSpec(memory_space=pltpu.VMEM)
    outs = [
        jax.ShapeDtypeStruct(shape, jnp.bfloat16) if final else pltpu.VMEM(shape, jnp.bfloat16)
        for shape in shapes
    ]
    moved = 2 * (sum(array.size for array in ins) + sum(math.prod(shape) for shape in shapes))
    return pl.pallas_call(
        kernel,
        in_specs=[vmem] * len(ins),
        out_specs=[vmem] * len(shapes),
        out_shape=outs,
        scratch_shapes=list(scratch),
        compiler_params=pltpu.CompilerParams(vmem_limit_bytes=ROOM),
        cost_estimate=pl.CostEstimate(flops=flops, bytes_accessed=moved, transcendentals=0),
    )(*ins)


def held(array):
    return pltpu.with_memory_space_constraint(array, pltpu.VMEM)


def where_am_i():
    me = lax.axis_index("wide")
    return me // 2, me % 2, lax.axis_index("narrow")


def project(mid_grad, link_weight, groups):
    rows, depth = mid_grad.shape
    features = link_weight.shape[0]
    patches, each = rows // PATCH, PATCH // groups

    def kernel(grad_ref, link_ref, stay_ref, leave_ref, product):
        side = where_am_i()[2]
        for low in range(0, features, 256):
            result = lax.dot_general(
                grad_ref[...],
                link_ref[low : low + 256],
                (((1,), (1,)), ((), ())),
                preferred_element_type=jnp.float32,
            )
            for slab in range(result.shape[1] // HD):
                product[low // HD + slab] = result[:, slab * HD : (slab + 1) * HD]
        for out, group in ((stay_ref, side), (leave_ref, 1 - side)):
            for index in range(each):
                for slab in range(features // HD):
                    at = index * features + slab * HD
                    picked = product[slab, pl.ds(group * each + index, patches, stride=PATCH), :]
                    out[:, at : at + HD] = picked.astype(jnp.bfloat16)

    return local(
        kernel,
        [mid_grad, link_weight],
        [(patches, each * features)] * 2,
        [pltpu.VMEM((features // HD, rows, HD), jnp.float32)],
        2 * rows * depth * features,
    )


def pack(arrays, chips, steps):
    rows, columns = arrays[0].shape
    wide = columns // chips

    def kernel(*refs):
        ins, outs = refs[: len(arrays)], refs[len(arrays) :]
        chip = where_am_i()[0]
        for out, step in zip(outs, steps):
            start = pl.multiple_of((chip ^ step) * wide, HD)
            for which, ref in enumerate(ins):
                out[:, which * wide : (which + 1) * wide] = ref[:, pl.ds(start, wide)]

    return local(kernel, arrays, [(rows, len(arrays) * wide)] * len(steps))


def pack_grads(arrays, stay, came, chips, steps, early):
    rows, columns = arrays[0].shape
    wide = columns // chips
    half = stay.shape[0]
    count = len(arrays)

    def kernel(*refs):
        ins, (stay_ref, came_ref) = refs[:count], refs[count : count + 2]
        outs, ordered = refs[count + 2 : -1], refs[-1]
        chip, _, side = where_am_i()
        mine, others = stay_ref[...].astype(jnp.float32), came_ref[...].astype(jnp.float32)
        ordered[:half] = jnp.where(side == 0, mine, others)
        ordered[half:] = jnp.where(side == 0, others, mine)
        for out, step in zip(outs, tuple(steps) + tuple(early)):
            start = pl.multiple_of((chip ^ step) * wide, HD)
            taken = ins if step in steps else ()
            for which, ref in enumerate(taken):
                out[:, which * wide : (which + 1) * wide] = ref[:, pl.ds(start, wide)]
            low = len(taken) * wide
            out[:, low : low + wide] = ordered[:, pl.ds(start, wide)].astype(jnp.bfloat16)

    return local(
        kernel,
        [*arrays, stay, came],
        [(rows, (count + 1) * wide)] * len(steps) + [(rows, wide)] * len(early),
        [pltpu.VMEM((rows, columns), jnp.float32)],
    )


def attend(own, other, rows):
    chips = len(own)
    total = 2 * chips * rows
    scaling = 1.0 / math.sqrt(HD)
    operands = [block for part in (own, other) for blocks in part for block in blocks]
    inputs = len(operands)

    def kernel(*refs):
        taken = iter(refs)
        own_refs, other_refs = (
            [[next(taken) for _ in blocks] for blocks in part] for part in (own, other)
        )
        outs = refs[inputs : inputs + chips]
        gathered, query_sum, key_sum, value_sum = refs[inputs + chips :]
        chip, core, _ = where_am_i()

        def piece(blocks, which, head):
            at = which * 3 + head
            if len(blocks) == 2 and which == 3:
                blocks, at = blocks[1:], head
            return blocks[0][:, pl.ds(pl.multiple_of(at * HD, HD), HD)].astype(jnp.float32)

        def spots(step):
            start = (chip ^ step) * (2 * rows)
            return (
                pl.ds(pl.multiple_of(start + core * rows, 8), rows),
                pl.ds(pl.multiple_of(start + (1 - core) * rows, 8), rows),
            )

        for index in range(2):
            head = core + index
            for which in range(4):
                for step in range(chips):
                    mine, others = spots(step)
                    gathered[which, mine, :] = piece(own_refs[step], which, head)
                    gathered[which, others, :] = piece(other_refs[step], which, head)
            query, keys, values, grads = (
                gathered[which].astype(jnp.bfloat16) for which in range(4)
            )
            for low in range(0, total, TILE):
                high = min(low + TILE, total)
                q, g = query[low:high], grads[low:high]
                k, v = keys[:high], values[:high]
                last = (((1,), (1,)), ((), ()))
                first = (((0,), (0,)), ((), ()))
                scores = scaling * lax.dot_general(q, k, last, preferred_element_type=jnp.float32)
                row = lax.broadcasted_iota(jnp.int32, scores.shape, 0) + low
                col = lax.broadcasted_iota(jnp.int32, scores.shape, 1)
                scores = jnp.where(col <= row, scores, lowest)
                expo = jnp.exp(scores - jnp.max(scores, axis=1, keepdims=True))
                products = lax.dot_general(g, v, last, preferred_element_type=jnp.float32)
                scale = 1.0 / jnp.sum(expo, axis=1, keepdims=True)
                delta = jnp.sum(expo * products, axis=1, keepdims=True) * scale
                weights = expo * scale
                score_grad = (weights * (products - delta)).astype(jnp.bfloat16)
                half = weights.astype(jnp.bfloat16)
                query_sum[low:high] = lax.dot_general(
                    score_grad, k, (((1,), (0,)), ((), ())), preferred_element_type=jnp.float32
                )
                key_part = lax.dot_general(score_grad, q, first, preferred_element_type=jnp.float32)
                value_part = lax.dot_general(half, g, first, preferred_element_type=jnp.float32)
                if low:
                    key_sum[:low] += key_part[:low]
                    value_sum[:low] += value_part[:low]
                key_sum[low:high] = key_part[low:]
                value_sum[low:high] = value_part[low:]
            for which, (store, factor) in enumerate(
                ((query_sum, scaling), (key_sum, scaling), (value_sum, 1.0))
            ):
                lanes = slice(which * HD, (which + 1) * HD)
                for step in range(chips):
                    mine, others = spots(step)

                    def rounded(spot):
                        return (store[spot] * factor).astype(jnp.bfloat16)

                    outs[step][pl.ds(jnp.where(head == 1, 1, 0), 1), :, lanes] = rounded(mine)[None]

                    @pl.when(head != 1)
                    def _():
                        outs[step][2, :, lanes] = rounded(others)

    big = pltpu.VMEM((total, HD), jnp.float32)
    return local(
        kernel,
        operands,
        [(3, rows, 3 * HD)] * chips,
        [pltpu.VMEM((4, total, HD), jnp.float32), big, big, big],
        10 * total * total * HD,
    )


def unpack(own, other, rows, columns):
    chips = len(own)
    wide = columns // chips

    def kernel(*refs):
        own_refs, other_refs, outs = refs[:chips], refs[chips : 2 * chips], refs[2 * chips :]
        chip, core, _ = where_am_i()
        for step in range(chips):
            start = (chip ^ step) * wide
            for which, out in enumerate(outs):
                lanes = slice(which * HD, (which + 1) * HD)

                def put(head, block):
                    out[:, pl.ds(pl.multiple_of(start + head * HD, HD), HD)] = block

                put(2 * core, own_refs[step][0, :, lanes])
                put(1, own_refs[step][1, :, lanes])
                put(2 - 2 * core, other_refs[step][2, :, lanes])

    return local(kernel, [*own, *other], [(rows, columns)] * 3, final=True)


def by_heads(query_rows, key_rows, value_rows, mid_grad, link_weight):
    rows, columns = query_rows.shape
    size = lax.axis_size("wide")
    chips = size // 2

    def cross(block, step):
        return held(lax.ppermute(block, "wide", [(i, i ^ step) for i in range(size)]))

    early, late = in_order(chips)
    arrays = [held(query_rows), held(key_rows), held(value_rows)]
    own = {}
    ahead = pack(arrays, chips, early) if early else []
    for step, block in zip(early, ahead):
        own[step] = [cross(block, 2 * step)]
    stay, leave = project(held(mid_grad), held(link_weight), 2)
    came = held(lax.ppermute(leave, "narrow", [(0, 1), (1, 0)]))
    rest = pack_grads(arrays, stay, came, chips, [0] + late, early)
    own[0] = [rest[0]]
    for step, block in zip(late, rest[1:]):
        own[step] = [cross(block, 2 * step)]
    for step, block in zip(early, rest[1 + len(late) :]):
        own[step].append(cross(block, 2 * step))
    own = [own[step] for step in range(chips)]
    other = [[cross(block, 1) for block in blocks] for blocks in own]
    done = attend(own, other, rows)
    own = [done[0]] + [cross(done[step], 2 * step) for step in range(1, chips)]
    other = [cross(block, 1) for block in own]
    return tuple(unpack(own, other, rows, columns))


def on_device(query_rows, key_rows, value_rows, mid_grad, link_weight):
    size = lax.axis_size("wide")
    rows, columns = query_rows.shape
    chips = size // 2
    fits = (
        size > 1
        and size & (size - 1) == 0
        and lax.axis_size("narrow") == 2
        and columns == chips * 3 * HD
        and (size * rows) % TILE == 0
        and rows % 8 == 0
    )
    plan = by_heads if fits else by_rows
    return plan(query_rows, key_rows, value_rows, mid_grad, link_weight)


def by_rows(query_rows, key_rows, value_rows, mid_grad, link_weight):
    groups = lax.axis_size("narrow")
    patches = query_rows.shape[0]
    columns = query_rows.shape[1]
    heads_here = columns // HD
    scaling = 1.0 / math.sqrt(HD)
    local_patches = mid_grad.shape[0] // PATCH
    grouped = mid_grad.reshape(local_patches, groups, PATCH // groups, mid_grad.shape[1])
    moved = jnp.einsum(
        "abcm,pm->abcp",
        lax.all_to_all(grouped, "narrow", split_axis=1, concat_axis=0, tiled=True),
        link_weight,
        preferred_element_type=jnp.float32,
    ).astype(jnp.bfloat16)
    incoming = moved.reshape(patches, columns)
    incoming_heads = incoming.reshape(patches, heads_here, HD)
    query_heads = query_rows.reshape(patches, heads_here, HD)
    key_heads = key_rows.reshape(patches, heads_here, HD)
    value_heads = value_rows.reshape(patches, heads_here, HD)
    own_pos = lax.axis_index("wide") * patches + jnp.arange(patches, dtype=jnp.int32)
    total_rows = patches * lax.axis_size("wide")
    empty_store = jnp.zeros((total_rows, columns), jnp.bfloat16)
    fold_start = (
        jnp.full((heads_here, patches), lowest, jnp.float32),
        jnp.zeros((heads_here, patches), jnp.float32),
        jnp.zeros((heads_here, patches), jnp.float32),
        empty_store,
        empty_store,
    )
    pieces = (
        lax.all_gather(key_rows, "wide", axis=0, tiled=True),
        lax.all_gather(value_rows, "wide", axis=0, tiled=True),
    )
    key_piece, value_piece = pieces
    piece_rows = key_piece.shape[0]
    key_split = key_piece.reshape(piece_rows, heads_here, HD)
    value_split = value_piece.reshape(piece_rows, heads_here, HD)
    piece_pos = jnp.arange(piece_rows, dtype=jnp.int32)
    allowed = piece_pos[None, None, :] <= own_pos[None, :, None]
    scores = (
        jnp.einsum("qhd,khd->hqk", query_heads, key_split, preferred_element_type=jnp.float32)
        * scaling
    )
    scores = jnp.where(allowed, scores, lowest)
    products = jnp.einsum(
        "qhd,khd->hqk", incoming_heads, value_split, preferred_element_type=jnp.float32
    )
    old_max, _, _ = fold_start[:3]
    new_max = jnp.maximum(old_max, jnp.max(scores, axis=2))
    expo = jnp.where(allowed, jnp.exp(scores - new_max[:, :, None]), 0.0)
    stats = (new_max, jnp.sum(expo, axis=2), jnp.sum(expo * products, axis=2))
    key_store = pieces[0]
    value_store = pieces[1]
    folded = stats + (key_store, value_store)
    run_max, run_total, run_tilt = (folded[0], folded[1], folded[2])
    log_total = run_max + jnp.log(run_total)
    row_delta = run_tilt / run_total
    key_all = folded[3].reshape(total_rows, heads_here, HD)
    value_all = folded[4].reshape(total_rows, heads_here, HD)
    every_pos = jnp.arange(total_rows, dtype=jnp.int32)
    allowed_q = every_pos[None, None, :] <= own_pos[None, :, None]
    scores_q = (
        jnp.einsum("qhd,khd->hqk", query_heads, key_all, preferred_element_type=jnp.float32)
        * scaling
    )
    products_q = jnp.einsum(
        "qhd,khd->hqk", incoming_heads, value_all, preferred_element_type=jnp.float32
    )
    weights_q = jnp.where(
        allowed_q, jnp.exp(jnp.where(allowed_q, scores_q, lowest) - log_total[:, :, None]), 0.0
    )
    score_grad_q = (weights_q * (products_q - row_delta[:, :, None])).astype(jnp.bfloat16)
    query_accum = jnp.einsum(
        "hqk,khd->qhd", score_grad_q, key_all, preferred_element_type=jnp.float32
    )
    query_grad = (query_accum * scaling).astype(jnp.bfloat16).reshape(patches, columns)
    total_all, delta_all = (
        lax.all_gather(log_total, "wide", axis=1, tiled=True),
        lax.all_gather(row_delta, "wide", axis=1, tiled=True),
    )
    query_piece = lax.all_gather(query_rows, "wide", axis=0, tiled=True)
    grad_piece = lax.all_gather(incoming, "wide", axis=0, tiled=True)
    piece_rows = query_piece.shape[0]
    query_split = query_piece.reshape(piece_rows, heads_here, HD)
    grad_split = grad_piece.reshape(piece_rows, heads_here, HD)
    piece_pos = jnp.arange(piece_rows, dtype=jnp.int32)
    allowed = own_pos[None, None, :] <= piece_pos[None, :, None]
    scores = (
        jnp.einsum("qhd,khd->hqk", query_split, key_heads, preferred_element_type=jnp.float32)
        * scaling
    )
    scores = jnp.where(allowed, scores, lowest)
    products = jnp.einsum(
        "qhd,khd->hqk", grad_split, value_heads, preferred_element_type=jnp.float32
    )
    weights = jnp.where(allowed, jnp.exp(scores - total_all[:, :, None]), 0.0)
    score_grad = (weights * (products - delta_all[:, :, None])).astype(jnp.bfloat16)
    key_accum = jnp.einsum(
        "hqk,qhd->khd", score_grad, query_split, preferred_element_type=jnp.float32
    )
    value_accum = jnp.einsum(
        "hqk,qhd->khd", weights.astype(jnp.bfloat16), grad_split, preferred_element_type=jnp.float32
    )
    key_accum, value_accum = (key_accum, value_accum)
    key_grad = (key_accum * scaling).astype(jnp.bfloat16).reshape(patches, columns)
    value_grad = value_accum.astype(jnp.bfloat16).reshape(patches, columns)
    return (query_grad, key_grad, value_grad)


def solution(mesh):
    in_specs = (
        P("wide", "narrow"),
        P("wide", "narrow"),
        P("wide", "narrow"),
        P(("wide", "narrow"), None),
        P(),
    )
    out_specs = (P("wide", "narrow"), P("wide", "narrow"), P("wide", "narrow"))
    return jax.shard_map(
        on_device, mesh=mesh, in_specs=in_specs, out_specs=out_specs, check_vma=False
    )
```

```python
import math

import jax
import jax.numpy as jnp
from jax import lax
from jax.experimental import pallas as pl
from jax.experimental.pallas import tpu as pltpu
from jax.sharding import PartitionSpec as P


HD = 128
PATCH = 8
TILE = 320
ROOM = 24 << 20


lowest = -1e30


def in_order(chips):
    far = list(range(chips // 2, chips))
    near = list(range(1, chips // 2))[::-1]
    return far[:2], far[2:] + near


def local(kernel, ins, shapes, scratch=(), flops=0, final=False, afar=()):
    vmem, anywhere = (pl.BlockSpec(memory_space=space) for space in (pltpu.VMEM, pltpu.HBM))
    outs = [
        jax.ShapeDtypeStruct(shape, jnp.bfloat16) if final else pltpu.VMEM(shape, jnp.bfloat16)
        for shape in shapes
    ]
    moved = 2 * (sum(array.size for array in ins) + sum(math.prod(shape) for shape in shapes))
    return pl.pallas_call(
        kernel,
        in_specs=[anywhere if i in afar else vmem for i in range(len(ins))],
        out_specs=[vmem] * len(shapes),
        out_shape=outs,
        scratch_shapes=list(scratch),
        compiler_params=pltpu.CompilerParams(vmem_limit_bytes=ROOM),
        cost_estimate=pl.CostEstimate(flops=flops, bytes_accessed=moved, transcendentals=0),
    )(*(pltpu.with_memory_space_constraint(x, pltpu.HBM) if i in afar else x for i, x in enumerate(ins)))


def held(array):
    return pltpu.with_memory_space_constraint(array, pltpu.VMEM)


def where_am_i():
    me = lax.axis_index("wide")
    return me // 2, me % 2, lax.axis_index("narrow")


def project(mid_grad, link_weight, groups):
    rows, depth = mid_grad.shape
    features = link_weight.shape[0]
    patches, each = rows // PATCH, PATCH // groups

    def kernel(grad_ref, link_ref, stay_ref, leave_ref, product):
        side = where_am_i()[2]
        for low in range(0, features, 256):
            result = lax.dot_general(
                grad_ref[...],
                link_ref[low : low + 256],
                (((1,), (1,)), ((), ())),
                preferred_element_type=jnp.float32,
            )
            for slab in range(result.shape[1] // HD):
                product[low // HD + slab] = result[:, slab * HD : (slab + 1) * HD]
        for out, group in ((stay_ref, side), (leave_ref, 1 - side)):
            for index in range(each):
                for slab in range(features // HD):
                    at = index * features + slab * HD
                    picked = product[slab, pl.ds(group * each + index, patches, stride=PATCH), :]
                    out[:, at : at + HD] = picked.astype(jnp.bfloat16)

    return local(
        kernel,
        [mid_grad, link_weight],
        [(patches, each * features)] * 2,
        [pltpu.VMEM((features // HD, rows, HD), jnp.float32)],
        2 * rows * depth * features,
    )


def pack(arrays, others, chips, steps):
    rows, columns = arrays[0].shape
    wide = columns // chips
    whole = [*arrays, *others]
    count = len(whole)

    def kernel(*refs):
        ins, kept, outs, arrived = refs[:count], refs[count : 2 * count], refs[2 * count : -1], refs[-1]
        copies = [
            pltpu.make_async_copy(ref, keep, arrived.at[which])
            for which, (ref, keep) in enumerate(zip(ins, kept))
        ]
        for copy in copies:
            copy.start()
        for copy in copies:
            copy.wait()
        chip = where_am_i()[0]
        for out, step in zip(outs, steps):
            start = pl.multiple_of((chip ^ step) * wide, HD)
            for which in range(len(arrays)):
                out[:, which * wide : (which + 1) * wide] = kept[which][:, pl.ds(start, wide)]

    return local(
        kernel,
        whole,
        [array.shape for array in whole] + [(rows, len(arrays) * wide)] * len(steps),
        [pltpu.SemaphoreType.DMA((count,))],
        flops=5 * 10**9,
        afar=range(count),
    )


def pack_grads(arrays, stay, came, chips, steps, early):
    rows, columns = arrays[0].shape
    wide = columns // chips
    half = stay.shape[0]
    count = len(arrays)

    def kernel(*refs):
        ins, (stay_ref, came_ref) = refs[:count], refs[count : count + 2]
        outs, ordered = refs[count + 2 : -1], refs[-1]
        chip, _, side = where_am_i()
        mine, others = stay_ref[...].astype(jnp.float32), came_ref[...].astype(jnp.float32)
        ordered[:half] = jnp.where(side == 0, mine, others)
        ordered[half:] = jnp.where(side == 0, others, mine)
        for out, step in zip(outs, tuple(steps) + tuple(early)):
            start = pl.multiple_of((chip ^ step) * wide, HD)
            taken = ins if step in steps else ()
            for which, ref in enumerate(taken):
                out[:, which * wide : (which + 1) * wide] = ref[:, pl.ds(start, wide)]
            low = len(taken) * wide
            out[:, low : low + wide] = ordered[:, pl.ds(start, wide)].astype(jnp.bfloat16)

    return local(
        kernel,
        [*arrays, stay, came],
        [(rows, (count + 1) * wide)] * len(steps) + [(rows, wide)] * len(early),
        [pltpu.VMEM((rows, columns), jnp.float32)],
    )


def attend(own, other, rows):
    chips = len(own)
    total = 2 * chips * rows
    scaling = 1.0 / math.sqrt(HD)
    operands = [block for part in (own, other) for blocks in part for block in blocks]
    inputs = len(operands)

    def kernel(*refs):
        taken = iter(refs)
        own_refs, other_refs = (
            [[next(taken) for _ in blocks] for blocks in part] for part in (own, other)
        )
        outs = refs[inputs : inputs + chips]
        gathered, query_sum, key_sum, value_sum = refs[inputs + chips :]
        chip, core, _ = where_am_i()

        def piece(blocks, which, head):
            at = which * 3 + head
            if len(blocks) == 2 and which == 3:
                blocks, at = blocks[1:], head
            return blocks[0][:, pl.ds(pl.multiple_of(at * HD, HD), HD)].astype(jnp.float32)

        def spots(step):
            start = (chip ^ step) * (2 * rows)
            return (
                pl.ds(pl.multiple_of(start + core * rows, 8), rows),
                pl.ds(pl.multiple_of(start + (1 - core) * rows, 8), rows),
            )

        for index in range(2):
            head = core + index
            for which in range(4):
                for step in range(chips):
                    mine, others = spots(step)
                    gathered[which, mine, :] = piece(own_refs[step], which, head)
                    gathered[which, others, :] = piece(other_refs[step], which, head)
            query, keys, values, grads = (
                gathered[which].astype(jnp.bfloat16) for which in range(4)
            )
            for low in range(0, total, TILE):
                high = min(low + TILE, total)
                q, g = query[low:high], grads[low:high]
                k, v = keys[:high], values[:high]
                last = (((1,), (1,)), ((), ()))
                first = (((0,), (0,)), ((), ()))
                scores = scaling * lax.dot_general(q, k, last, preferred_element_type=jnp.float32)
                row = lax.broadcasted_iota(jnp.int32, scores.shape, 0) + low
                col = lax.broadcasted_iota(jnp.int32, scores.shape, 1)
                scores = jnp.where(col <= row, scores, lowest)
                expo = jnp.exp(scores - jnp.max(scores, axis=1, keepdims=True))
                products = lax.dot_general(g, v, last, preferred_element_type=jnp.float32)
                scale = 1.0 / jnp.sum(expo, axis=1, keepdims=True)
                delta = jnp.sum(expo * products, axis=1, keepdims=True) * scale
                weights = expo * scale
                score_grad = (weights * (products - delta)).astype(jnp.bfloat16)
                half = weights.astype(jnp.bfloat16)
                query_sum[low:high] = lax.dot_general(
                    score_grad, k, (((1,), (0,)), ((), ())), preferred_element_type=jnp.float32
                )
                key_part = lax.dot_general(score_grad, q, first, preferred_element_type=jnp.float32)
                value_part = lax.dot_general(half, g, first, preferred_element_type=jnp.float32)
                if low:
                    key_sum[:low] += key_part[:low]
                    value_sum[:low] += value_part[:low]
                key_sum[low:high] = key_part[low:]
                value_sum[low:high] = value_part[low:]
            for which, (store, factor) in enumerate(
                ((query_sum, scaling), (key_sum, scaling), (value_sum, 1.0))
            ):
                lanes = slice(which * HD, (which + 1) * HD)
                for step in range(chips):
                    mine, others = spots(step)

                    def rounded(spot):
                        return (store[spot] * factor).astype(jnp.bfloat16)

                    outs[step][pl.ds(jnp.where(head == 1, 1, 0), 1), :, lanes] = rounded(mine)[None]

                    @pl.when(head != 1)
                    def _():
                        outs[step][2, :, lanes] = rounded(others)

    big = pltpu.VMEM((total, HD), jnp.float32)
    return local(
        kernel,
        operands,
        [(3, rows, 3 * HD)] * chips,
        [pltpu.VMEM((4, total, HD), jnp.float32), big, big, big],
        10 * total * total * HD,
    )


def unpack(own, other, rows, columns):
    chips = len(own)
    wide = columns // chips

    def kernel(*refs):
        own_refs, other_refs, outs = refs[:chips], refs[chips : 2 * chips], refs[2 * chips :]
        chip, core, _ = where_am_i()
        for step in range(chips):
            start = (chip ^ step) * wide
            for which, out in enumerate(outs):
                lanes = slice(which * HD, (which + 1) * HD)

                def put(head, block):
                    out[:, pl.ds(pl.multiple_of(start + head * HD, HD), HD)] = block

                put(2 * core, own_refs[step][0, :, lanes])
                put(1, own_refs[step][1, :, lanes])
                put(2 - 2 * core, other_refs[step][2, :, lanes])

    return local(kernel, [*own, *other], [(rows, columns)] * 3, final=True)


def by_heads(query_rows, key_rows, value_rows, mid_grad, link_weight):
    rows, columns = query_rows.shape
    size = lax.axis_size("wide")
    chips = size // 2

    def cross(block, step):
        return held(lax.ppermute(block, "wide", [(i, i ^ step) for i in range(size)]))

    early, late = in_order(chips)
    own = {}
    ahead = pack([query_rows, key_rows, value_rows], [], chips, early)
    arrays, ahead = ahead[:3], ahead[3:]
    for step, block in zip(early, ahead):
        own[step] = [cross(block, 2 * step)]
    stay, leave = project(mid_grad, link_weight, 2)
    came = held(lax.ppermute(leave, "narrow", [(0, 1), (1, 0)]))
    rest = pack_grads(arrays, stay, came, chips, [0] + late, early)
    own[0] = [rest[0]]
    for step, block in zip(late, rest[1:]):
        own[step] = [cross(block, 2 * step)]
    for step, block in zip(early, rest[1 + len(late) :]):
        own[step].append(cross(block, 2 * step))
    own = [own[step] for step in range(chips)]
    other = [[cross(block, 1) for block in blocks] for blocks in own]
    done = attend(own, other, rows)
    own = [done[0]] + [cross(done[step], 2 * step) for step in range(1, chips)]
    other = [cross(block, 1) for block in own]
    return tuple(unpack(own, other, rows, columns))


def on_device(query_rows, key_rows, value_rows, mid_grad, link_weight):
    size = lax.axis_size("wide")
    rows, columns = query_rows.shape
    chips = size // 2
    fits = (
        size > 1
        and size & (size - 1) == 0
        and lax.axis_size("narrow") == 2
        and columns == chips * 3 * HD
        and (size * rows) % TILE == 0
        and rows % 8 == 0
    )
    plan = by_heads if fits else by_rows
    return plan(query_rows, key_rows, value_rows, mid_grad, link_weight)


def by_rows(query_rows, key_rows, value_rows, mid_grad, link_weight):
    groups = lax.axis_size("narrow")
    patches = query_rows.shape[0]
    columns = query_rows.shape[1]
    heads_here = columns // HD
    scaling = 1.0 / math.sqrt(HD)
    local_patches = mid_grad.shape[0] // PATCH
    grouped = mid_grad.reshape(local_patches, groups, PATCH // groups, mid_grad.shape[1])
    moved = jnp.einsum(
        "abcm,pm->abcp",
        lax.all_to_all(grouped, "narrow", split_axis=1, concat_axis=0, tiled=True),
        link_weight,
        preferred_element_type=jnp.float32,
    ).astype(jnp.bfloat16)
    incoming = moved.reshape(patches, columns)
    incoming_heads = incoming.reshape(patches, heads_here, HD)
    query_heads = query_rows.reshape(patches, heads_here, HD)
    key_heads = key_rows.reshape(patches, heads_here, HD)
    value_heads = value_rows.reshape(patches, heads_here, HD)
    own_pos = lax.axis_index("wide") * patches + jnp.arange(patches, dtype=jnp.int32)
    total_rows = patches * lax.axis_size("wide")
    empty_store = jnp.zeros((total_rows, columns), jnp.bfloat16)
    fold_start = (
        jnp.full((heads_here, patches), lowest, jnp.float32),
        jnp.zeros((heads_here, patches), jnp.float32),
        jnp.zeros((heads_here, patches), jnp.float32),
        empty_store,
        empty_store,
    )
    pieces = (
        lax.all_gather(key_rows, "wide", axis=0, tiled=True),
        lax.all_gather(value_rows, "wide", axis=0, tiled=True),
    )
    key_piece, value_piece = pieces
    piece_rows = key_piece.shape[0]
    key_split = key_piece.reshape(piece_rows, heads_here, HD)
    value_split = value_piece.reshape(piece_rows, heads_here, HD)
    piece_pos = jnp.arange(piece_rows, dtype=jnp.int32)
    allowed = piece_pos[None, None, :] <= own_pos[None, :, None]
    scores = (
        jnp.einsum("qhd,khd->hqk", query_heads, key_split, preferred_element_type=jnp.float32)
        * scaling
    )
    scores = jnp.where(allowed, scores, lowest)
    products = jnp.einsum(
        "qhd,khd->hqk", incoming_heads, value_split, preferred_element_type=jnp.float32
    )
    old_max, _, _ = fold_start[:3]
    new_max = jnp.maximum(old_max, jnp.max(scores, axis=2))
    expo = jnp.where(allowed, jnp.exp(scores - new_max[:, :, None]), 0.0)
    stats = (new_max, jnp.sum(expo, axis=2), jnp.sum(expo * products, axis=2))
    key_store = pieces[0]
    value_store = pieces[1]
    folded = stats + (key_store, value_store)
    run_max, run_total, run_tilt = (folded[0], folded[1], folded[2])
    log_total = run_max + jnp.log(run_total)
    row_delta = run_tilt / run_total
    key_all = folded[3].reshape(total_rows, heads_here, HD)
    value_all = folded[4].reshape(total_rows, heads_here, HD)
    every_pos = jnp.arange(total_rows, dtype=jnp.int32)
    allowed_q = every_pos[None, None, :] <= own_pos[None, :, None]
    scores_q = (
        jnp.einsum("qhd,khd->hqk", query_heads, key_all, preferred_element_type=jnp.float32)
        * scaling
    )
    products_q = jnp.einsum(
        "qhd,khd->hqk", incoming_heads, value_all, preferred_element_type=jnp.float32
    )
    weights_q = jnp.where(
        allowed_q, jnp.exp(jnp.where(allowed_q, scores_q, lowest) - log_total[:, :, None]), 0.0
    )
    score_grad_q = (weights_q * (products_q - row_delta[:, :, None])).astype(jnp.bfloat16)
    query_accum = jnp.einsum(
        "hqk,khd->qhd", score_grad_q, key_all, preferred_element_type=jnp.float32
    )
    query_grad = (query_accum * scaling).astype(jnp.bfloat16).reshape(patches, columns)
    total_all, delta_all = (
        lax.all_gather(log_total, "wide", axis=1, tiled=True),
        lax.all_gather(row_delta, "wide", axis=1, tiled=True),
    )
    query_piece = lax.all_gather(query_rows, "wide", axis=0, tiled=True)
    grad_piece = lax.all_gather(incoming, "wide", axis=0, tiled=True)
    piece_rows = query_piece.shape[0]
    query_split = query_piece.reshape(piece_rows, heads_here, HD)
    grad_split = grad_piece.reshape(piece_rows, heads_here, HD)
    piece_pos = jnp.arange(piece_rows, dtype=jnp.int32)
    allowed = own_pos[None, None, :] <= piece_pos[None, :, None]
    scores = (
        jnp.einsum("qhd,khd->hqk", query_split, key_heads, preferred_element_type=jnp.float32)
        * scaling
    )
    scores = jnp.where(allowed, scores, lowest)
    products = jnp.einsum(
        "qhd,khd->hqk", grad_split, value_heads, preferred_element_type=jnp.float32
    )
    weights = jnp.where(allowed, jnp.exp(scores - total_all[:, :, None]), 0.0)
    score_grad = (weights * (products - delta_all[:, :, None])).astype(jnp.bfloat16)
    key_accum = jnp.einsum(
        "hqk,qhd->khd", score_grad, query_split, preferred_element_type=jnp.float32
    )
    value_accum = jnp.einsum(
        "hqk,qhd->khd", weights.astype(jnp.bfloat16), grad_split, preferred_element_type=jnp.float32
    )
    key_accum, value_accum = (key_accum, value_accum)
    key_grad = (key_accum * scaling).astype(jnp.bfloat16).reshape(patches, columns)
    value_grad = value_accum.astype(jnp.bfloat16).reshape(patches, columns)
    return (query_grad, key_grad, value_grad)


def solution(mesh):
    in_specs = (
        P("wide", "narrow"),
        P("wide", "narrow"),
        P("wide", "narrow"),
        P(("wide", "narrow"), None),
        P(),
    )
    out_specs = (P("wide", "narrow"), P("wide", "narrow"), P("wide", "narrow"))
    return jax.shard_map(
        on_device, mesh=mesh, in_specs=in_specs, out_specs=out_specs, check_vma=False
    )
```

```python
import math

import jax
import jax.numpy as jnp
from jax import lax
from jax.experimental import pallas as pl
from jax.experimental.pallas import tpu as pltpu
from jax.sharding import PartitionSpec as P


HD = 128
PATCH = 8
TILE = 320
ROOM = 24 << 20


lowest = -1e30


def in_order(chips):
    far, near = far_and_near(chips)
    return far[:3], far[3:] + near


def far_and_near(chips):
    return list(range(chips // 2, chips)), list(range(1, chips // 2))[::-1]


def local(kernel, ins, shapes, scratch=(), flops=0, final=False, afar=()):
    vmem, anywhere = (pl.BlockSpec(memory_space=space) for space in (pltpu.VMEM, pltpu.HBM))
    outs = [
        jax.ShapeDtypeStruct(shape, jnp.bfloat16) if final else pltpu.VMEM(shape, jnp.bfloat16)
        for shape in shapes
    ]
    moved = 2 * (sum(array.size for array in ins) + sum(math.prod(shape) for shape in shapes))
    return pl.pallas_call(
        kernel,
        in_specs=[anywhere if i in afar else vmem for i in range(len(ins))],
        out_specs=[vmem] * len(shapes),
        out_shape=outs,
        scratch_shapes=list(scratch),
        compiler_params=pltpu.CompilerParams(vmem_limit_bytes=ROOM),
        cost_estimate=pl.CostEstimate(flops=flops, bytes_accessed=moved, transcendentals=0),
    )(*(pltpu.with_memory_space_constraint(x, pltpu.HBM) if i in afar else x for i, x in enumerate(ins)))


def held(array):
    return pltpu.with_memory_space_constraint(array, pltpu.VMEM)


def where_am_i():
    me = lax.axis_index("wide")
    return me // 2, me % 2, lax.axis_index("narrow")


def project(mid_grad, link_weight, groups):
    rows, depth = mid_grad.shape
    features = link_weight.shape[0]
    patches, each = rows // PATCH, PATCH // groups

    def kernel(grad_ref, link_ref, stay_ref, leave_ref, product):
        side = where_am_i()[2]
        for low in range(0, features, 256):
            result = lax.dot_general(
                grad_ref[...],
                link_ref[low : low + 256],
                (((1,), (1,)), ((), ())),
                preferred_element_type=jnp.float32,
            )
            for slab in range(result.shape[1] // HD):
                product[low // HD + slab] = result[:, slab * HD : (slab + 1) * HD]
        for out, group in ((stay_ref, side), (leave_ref, 1 - side)):
            for index in range(each):
                for slab in range(features // HD):
                    at = index * features + slab * HD
                    picked = product[slab, pl.ds(group * each + index, patches, stride=PATCH), :]
                    out[:, at : at + HD] = picked.astype(jnp.bfloat16)

    return local(
        kernel,
        [mid_grad, link_weight],
        [(patches, each * features)] * 2,
        [pltpu.VMEM((features // HD, rows, HD), jnp.float32)],
        2 * rows * depth * features,
    )


def pack(arrays, chips, steps, first=False):
    rows, columns = arrays[0].shape
    wide = columns // chips
    count = len(arrays)

    def kernel(*refs):
        ins, outs = refs[:count], refs[count : count + len(steps)]
        chip = where_am_i()[0]
        copies = []
        for at, (out, step) in enumerate(zip(outs, steps)):
            start = pl.multiple_of((chip ^ step) * wide, HD)
            for which, ref in enumerate(ins):
                source, target = ref.at[:, pl.ds(start, wide)], out.at[:, which * wide : (which + 1) * wide]
                if first:
                    arrived = refs[-1].at[at * count + which]
                    copies.append(pltpu.make_async_copy(source, target, arrived))
                    copies[-1].start()
                else:
                    target[...] = source[...]
        for copy in copies:
            copy.wait()

    return local(
        kernel,
        arrays,
        [(rows, count * wide)] * len(steps),
        [pltpu.SemaphoreType.DMA((count * len(steps),))] if first else (),
        flops=5 * 10**9 if first else 0,
        afar=range(count) if first else (),
    )


def pack_grads(arrays, stay, came, chips, steps, early):
    rows, columns = arrays[0].shape
    wide = columns // chips
    half = stay.shape[0]
    count = len(arrays)

    def kernel(*refs):
        ins, (stay_ref, came_ref) = refs[:count], refs[count : count + 2]
        outs, ordered = refs[count + 2 : -1], refs[-1]
        chip, _, side = where_am_i()
        mine, others = stay_ref[...].astype(jnp.float32), came_ref[...].astype(jnp.float32)
        ordered[:half] = jnp.where(side == 0, mine, others)
        ordered[half:] = jnp.where(side == 0, others, mine)
        for out, step in zip(outs, tuple(steps) + tuple(early)):
            start = pl.multiple_of((chip ^ step) * wide, HD)
            taken = ins if step in steps else ()
            for which, ref in enumerate(taken):
                out[:, which * wide : (which + 1) * wide] = ref[:, pl.ds(start, wide)]
            low = len(taken) * wide
            out[:, low : low + wide] = ordered[:, pl.ds(start, wide)].astype(jnp.bfloat16)

    return local(
        kernel,
        [*arrays, stay, came],
        [(rows, (count + 1) * wide)] * len(steps) + [(rows, wide)] * len(early),
        [pltpu.VMEM((rows, columns), jnp.float32)],
    )


def attend(own, other, rows):
    chips = len(own)
    total = 2 * chips * rows
    scaling = 1.0 / math.sqrt(HD)
    operands = [block for part in (own, other) for blocks in part for block in blocks]
    inputs = len(operands)

    def kernel(*refs):
        taken = iter(refs)
        own_refs, other_refs = (
            [[next(taken) for _ in blocks] for blocks in part] for part in (own, other)
        )
        outs = refs[inputs : inputs + chips]
        gathered, query_sum, key_sum, value_sum = refs[inputs + chips :]
        chip, core, _ = where_am_i()

        def piece(blocks, which, head):
            at = which * 3 + head
            if len(blocks) == 2 and which == 3:
                blocks, at = blocks[1:], head
            return blocks[0][:, pl.ds(pl.multiple_of(at * HD, HD), HD)].astype(jnp.float32)

        def spots(step):
            start = (chip ^ step) * (2 * rows)
            return (
                pl.ds(pl.multiple_of(start + core * rows, 8), rows),
                pl.ds(pl.multiple_of(start + (1 - core) * rows, 8), rows),
            )

        for index in range(2):
            head = core + index
            for which in range(4):
                for step in range(chips):
                    mine, others = spots(step)
                    gathered[which, mine, :] = piece(own_refs[step], which, head)
                    gathered[which, others, :] = piece(other_refs[step], which, head)
            query, keys, values, grads = (
                gathered[which].astype(jnp.bfloat16) for which in range(4)
            )
            for low in range(0, total, TILE):
                high = min(low + TILE, total)
                q, g = query[low:high], grads[low:high]
                k, v = keys[:high], values[:high]
                last = (((1,), (1,)), ((), ()))
                first = (((0,), (0,)), ((), ()))
                scores = scaling * lax.dot_general(q, k, last, preferred_element_type=jnp.float32)
                row = lax.broadcasted_iota(jnp.int32, scores.shape, 0) + low
                col = lax.broadcasted_iota(jnp.int32, scores.shape, 1)
                scores = jnp.where(col <= row, scores, lowest)
                expo = jnp.exp(scores - jnp.max(scores, axis=1, keepdims=True))
                products = lax.dot_general(g, v, last, preferred_element_type=jnp.float32)
                scale = 1.0 / jnp.sum(expo, axis=1, keepdims=True)
                delta = jnp.sum(expo * products, axis=1, keepdims=True) * scale
                weights = expo * scale
                score_grad = (weights * (products - delta)).astype(jnp.bfloat16)
                half = weights.astype(jnp.bfloat16)
                query_sum[low:high] = lax.dot_general(
                    score_grad, k, (((1,), (0,)), ((), ())), preferred_element_type=jnp.float32
                )
                key_part = lax.dot_general(score_grad, q, first, preferred_element_type=jnp.float32)
                value_part = lax.dot_general(half, g, first, preferred_element_type=jnp.float32)
                if low:
                    key_sum[:low] += key_part[:low]
                    value_sum[:low] += value_part[:low]
                key_sum[low:high] = key_part[low:]
                value_sum[low:high] = value_part[low:]
            for which, (store, factor) in enumerate(
                ((query_sum, scaling), (key_sum, scaling), (value_sum, 1.0))
            ):
                lanes = slice(which * HD, (which + 1) * HD)
                for step in range(chips):
                    mine, others = spots(step)

                    def rounded(spot):
                        return (store[spot] * factor).astype(jnp.bfloat16)

                    outs[step][pl.ds(jnp.where(head == 1, 1, 0), 1), :, lanes] = rounded(mine)[None]

                    @pl.when(head != 1)
                    def _():
                        outs[step][2, :, lanes] = rounded(others)

    big = pltpu.VMEM((total, HD), jnp.float32)
    return local(
        kernel,
        operands,
        [(3, rows, 3 * HD)] * chips,
        [pltpu.VMEM((4, total, HD), jnp.float32), big, big, big],
        10 * total * total * HD,
    )


def unpack(own, other, rows, columns):
    chips = len(own)
    wide = columns // chips

    def kernel(*refs):
        own_refs, other_refs, outs = refs[:chips], refs[chips : 2 * chips], refs[2 * chips :]
        chip, core, _ = where_am_i()
        for step in range(chips):
            start = (chip ^ step) * wide
            for which, out in enumerate(outs):
                lanes = slice(which * HD, (which + 1) * HD)

                def put(head, block):
                    out[:, pl.ds(pl.multiple_of(start + head * HD, HD), HD)] = block

                put(2 * core, own_refs[step][0, :, lanes])
                put(1, own_refs[step][1, :, lanes])
                put(2 - 2 * core, other_refs[step][2, :, lanes])

    return local(kernel, [*own, *other], [(rows, columns)] * 3, final=True)


def by_heads(query_rows, key_rows, value_rows, mid_grad, link_weight):
    rows, columns = query_rows.shape
    size = lax.axis_size("wide")
    chips = size // 2

    def cross(block, step):
        return held(lax.ppermute(block, "wide", [(i, i ^ step) for i in range(size)]))

    early, late = in_order(chips)
    own = {}
    arrays = [query_rows, key_rows, value_rows]
    ahead = pack(arrays, chips, early[:1], first=True)
    ahead += pack(arrays, chips, early[1:]) if early[1:] else []
    for step, block in zip(early, ahead):
        own[step] = [cross(block, 2 * step)]
    stay, leave = project(mid_grad, link_weight, 2)
    came = held(lax.ppermute(leave, "narrow", [(0, 1), (1, 0)]))
    rest = pack_grads(arrays, stay, came, chips, [0] + late, early)
    own[0] = [rest[0]]
    for step, block in zip(late, rest[1:]):
        own[step] = [cross(block, 2 * step)]
    for step, block in zip(early, rest[1 + len(late) :]):
        own[step].append(cross(block, 2 * step))
    own = [own[step] for step in range(chips)]
    other = [[cross(block, 1) for block in blocks] for blocks in own]
    done = attend(own, other, rows)
    own = [done[0]] + [cross(done[step], 2 * step) for step in range(1, chips)]
    other = [cross(block, 1) for block in own]
    return tuple(unpack(own, other, rows, columns))


def on_device(query_rows, key_rows, value_rows, mid_grad, link_weight):
    size = lax.axis_size("wide")
    rows, columns = query_rows.shape
    chips = size // 2
    fits = (
        size > 1
        and size & (size - 1) == 0
        and lax.axis_size("narrow") == 2
        and columns == chips * 3 * HD
        and (size * rows) % TILE == 0
        and rows % 8 == 0
    )
    plan = by_heads if fits else by_rows
    return plan(query_rows, key_rows, value_rows, mid_grad, link_weight)


def by_rows(query_rows, key_rows, value_rows, mid_grad, link_weight):
    groups = lax.axis_size("narrow")
    patches = query_rows.shape[0]
    columns = query_rows.shape[1]
    heads_here = columns // HD
    scaling = 1.0 / math.sqrt(HD)
    local_patches = mid_grad.shape[0] // PATCH
    grouped = mid_grad.reshape(local_patches, groups, PATCH // groups, mid_grad.shape[1])
    moved = jnp.einsum(
        "abcm,pm->abcp",
        lax.all_to_all(grouped, "narrow", split_axis=1, concat_axis=0, tiled=True),
        link_weight,
        preferred_element_type=jnp.float32,
    ).astype(jnp.bfloat16)
    incoming = moved.reshape(patches, columns)
    incoming_heads = incoming.reshape(patches, heads_here, HD)
    query_heads = query_rows.reshape(patches, heads_here, HD)
    key_heads = key_rows.reshape(patches, heads_here, HD)
    value_heads = value_rows.reshape(patches, heads_here, HD)
    own_pos = lax.axis_index("wide") * patches + jnp.arange(patches, dtype=jnp.int32)
    total_rows = patches * lax.axis_size("wide")
    empty_store = jnp.zeros((total_rows, columns), jnp.bfloat16)
    fold_start = (
        jnp.full((heads_here, patches), lowest, jnp.float32),
        jnp.zeros((heads_here, patches), jnp.float32),
        jnp.zeros((heads_here, patches), jnp.float32),
        empty_store,
        empty_store,
    )
    pieces = (
        lax.all_gather(key_rows, "wide", axis=0, tiled=True),
        lax.all_gather(value_rows, "wide", axis=0, tiled=True),
    )
    key_piece, value_piece = pieces
    piece_rows = key_piece.shape[0]
    key_split = key_piece.reshape(piece_rows, heads_here, HD)
    value_split = value_piece.reshape(piece_rows, heads_here, HD)
    piece_pos = jnp.arange(piece_rows, dtype=jnp.int32)
    allowed = piece_pos[None, None, :] <= own_pos[None, :, None]
    scores = (
        jnp.einsum("qhd,khd->hqk", query_heads, key_split, preferred_element_type=jnp.float32)
        * scaling
    )
    scores = jnp.where(allowed, scores, lowest)
    products = jnp.einsum(
        "qhd,khd->hqk", incoming_heads, value_split, preferred_element_type=jnp.float32
    )
    old_max, _, _ = fold_start[:3]
    new_max = jnp.maximum(old_max, jnp.max(scores, axis=2))
    expo = jnp.where(allowed, jnp.exp(scores - new_max[:, :, None]), 0.0)
    stats = (new_max, jnp.sum(expo, axis=2), jnp.sum(expo * products, axis=2))
    key_store = pieces[0]
    value_store = pieces[1]
    folded = stats + (key_store, value_store)
    run_max, run_total, run_tilt = (folded[0], folded[1], folded[2])
    log_total = run_max + jnp.log(run_total)
    row_delta = run_tilt / run_total
    key_all = folded[3].reshape(total_rows, heads_here, HD)
    value_all = folded[4].reshape(total_rows, heads_here, HD)
    every_pos = jnp.arange(total_rows, dtype=jnp.int32)
    allowed_q = every_pos[None, None, :] <= own_pos[None, :, None]
    scores_q = (
        jnp.einsum("qhd,khd->hqk", query_heads, key_all, preferred_element_type=jnp.float32)
        * scaling
    )
    products_q = jnp.einsum(
        "qhd,khd->hqk", incoming_heads, value_all, preferred_element_type=jnp.float32
    )
    weights_q = jnp.where(
        allowed_q, jnp.exp(jnp.where(allowed_q, scores_q, lowest) - log_total[:, :, None]), 0.0
    )
    score_grad_q = (weights_q * (products_q - row_delta[:, :, None])).astype(jnp.bfloat16)
    query_accum = jnp.einsum(
        "hqk,khd->qhd", score_grad_q, key_all, preferred_element_type=jnp.float32
    )
    query_grad = (query_accum * scaling).astype(jnp.bfloat16).reshape(patches, columns)
    total_all, delta_all = (
        lax.all_gather(log_total, "wide", axis=1, tiled=True),
        lax.all_gather(row_delta, "wide", axis=1, tiled=True),
    )
    query_piece = lax.all_gather(query_rows, "wide", axis=0, tiled=True)
    grad_piece = lax.all_gather(incoming, "wide", axis=0, tiled=True)
    piece_rows = query_piece.shape[0]
    query_split = query_piece.reshape(piece_rows, heads_here, HD)
    grad_split = grad_piece.reshape(piece_rows, heads_here, HD)
    piece_pos = jnp.arange(piece_rows, dtype=jnp.int32)
    allowed = own_pos[None, None, :] <= piece_pos[None, :, None]
    scores = (
        jnp.einsum("qhd,khd->hqk", query_split, key_heads, preferred_element_type=jnp.float32)
        * scaling
    )
    scores = jnp.where(allowed, scores, lowest)
    products = jnp.einsum(
        "qhd,khd->hqk", grad_split, value_heads, preferred_element_type=jnp.float32
    )
    weights = jnp.where(allowed, jnp.exp(scores - total_all[:, :, None]), 0.0)
    score_grad = (weights * (products - delta_all[:, :, None])).astype(jnp.bfloat16)
    key_accum = jnp.einsum(
        "hqk,qhd->khd", score_grad, query_split, preferred_element_type=jnp.float32
    )
    value_accum = jnp.einsum(
        "hqk,qhd->khd", weights.astype(jnp.bfloat16), grad_split, preferred_element_type=jnp.float32
    )
    key_accum, value_accum = (key_accum, value_accum)
    key_grad = (key_accum * scaling).astype(jnp.bfloat16).reshape(patches, columns)
    value_grad = value_accum.astype(jnp.bfloat16).reshape(patches, columns)
    return (query_grad, key_grad, value_grad)


def solution(mesh):
    in_specs = (
        P("wide", "narrow"),
        P("wide", "narrow"),
        P("wide", "narrow"),
        P(("wide", "narrow"), None),
        P(),
    )
    out_specs = (P("wide", "narrow"), P("wide", "narrow"), P("wide", "narrow"))
    return jax.shard_map(
        on_device, mesh=mesh, in_specs=in_specs, out_specs=out_specs, check_vma=False
    )
```

```python
import math

import jax
import jax.numpy as jnp
from jax import lax
from jax.experimental import pallas as pl
from jax.experimental.pallas import tpu as pltpu
from jax.sharding import PartitionSpec as P


HD = 128
PATCH = 8
ROOM = 24 << 20


lowest = -1e30


def in_order(chips):
    far, near = far_and_near(chips)
    return far[:3], far[3:] + near


def far_and_near(chips):
    return list(range(chips // 2, chips)), list(range(1, chips // 2))[::-1]


def local(kernel, ins, shapes, scratch=(), flops=0, final=False, afar=()):
    vmem, anywhere = (pl.BlockSpec(memory_space=space) for space in (pltpu.VMEM, pltpu.HBM))
    outs = [
        jax.ShapeDtypeStruct(shape, jnp.bfloat16) if final else pltpu.VMEM(shape, jnp.bfloat16)
        for shape in shapes
    ]
    moved = 2 * (sum(array.size for array in ins) + sum(math.prod(shape) for shape in shapes))
    return pl.pallas_call(
        kernel,
        in_specs=[anywhere if i in afar else vmem for i in range(len(ins))],
        out_specs=[vmem] * len(shapes),
        out_shape=outs,
        scratch_shapes=list(scratch),
        compiler_params=pltpu.CompilerParams(vmem_limit_bytes=ROOM),
        cost_estimate=pl.CostEstimate(flops=flops, bytes_accessed=moved, transcendentals=0),
    )(*(pltpu.with_memory_space_constraint(x, pltpu.HBM) if i in afar else x for i, x in enumerate(ins)))


def held(array):
    return pltpu.with_memory_space_constraint(array, pltpu.VMEM)


def where_am_i():
    me = lax.axis_index("wide")
    return me // 2, me % 2, lax.axis_index("narrow")


def project(mid_grad, link_weight, groups):
    rows, depth = mid_grad.shape
    features = link_weight.shape[0]
    patches, each = rows // PATCH, PATCH // groups

    def kernel(grad_ref, link_ref, stay_ref, leave_ref, product):
        side = where_am_i()[2]
        for low in range(0, features, 256):
            result = lax.dot_general(
                grad_ref[...],
                link_ref[low : low + 256],
                (((1,), (1,)), ((), ())),
                preferred_element_type=jnp.float32,
            )
            for slab in range(result.shape[1] // HD):
                product[low // HD + slab] = result[:, slab * HD : (slab + 1) * HD]
        for out, group in ((stay_ref, side), (leave_ref, 1 - side)):
            for index in range(each):
                for slab in range(features // HD):
                    at = index * features + slab * HD
                    picked = product[slab, pl.ds(group * each + index, patches, stride=PATCH), :]
                    out[:, at : at + HD] = picked.astype(jnp.bfloat16)

    return local(
        kernel,
        [mid_grad, link_weight],
        [(patches, each * features)] * 2,
        [pltpu.VMEM((features // HD, rows, HD), jnp.float32)],
        2 * rows * depth * features,
    )


def pack(arrays, chips, steps, first=False):
    rows, columns = arrays[0].shape
    wide = columns // chips
    count = len(arrays)

    def kernel(*refs):
        ins, outs = refs[:count], refs[count : count + len(steps)]
        chip = where_am_i()[0]
        copies = []
        for at, (out, step) in enumerate(zip(outs, steps)):
            start = pl.multiple_of((chip ^ step) * wide, HD)
            for which, ref in enumerate(ins):
                source, target = ref.at[:, pl.ds(start, wide)], out.at[:, which * wide : (which + 1) * wide]
                if first:
                    arrived = refs[-1].at[at * count + which]
                    copies.append(pltpu.make_async_copy(source, target, arrived))
                    copies[-1].start()
                else:
                    target[...] = source[...]
        for copy in copies:
            copy.wait()

    return local(
        kernel,
        arrays,
        [(rows, count * wide)] * len(steps),
        [pltpu.SemaphoreType.DMA((count * len(steps),))] if first else (),
        flops=5 * 10**9 if first else 0,
        afar=range(count) if first else (),
    )


def pack_grads(arrays, stay, came, chips, steps, early):
    rows, columns = arrays[0].shape
    wide = columns // chips
    half = stay.shape[0]
    count = len(arrays)

    def kernel(*refs):
        ins, (stay_ref, came_ref) = refs[:count], refs[count : count + 2]
        outs, ordered = refs[count + 2 : -1], refs[-1]
        chip, _, side = where_am_i()
        mine, others = stay_ref[...].astype(jnp.float32), came_ref[...].astype(jnp.float32)
        ordered[:half] = jnp.where(side == 0, mine, others)
        ordered[half:] = jnp.where(side == 0, others, mine)
        for out, step in zip(outs, tuple(steps) + tuple(early)):
            start = pl.multiple_of((chip ^ step) * wide, HD)
            taken = ins if step in steps else ()
            for which, ref in enumerate(taken):
                out[:, which * wide : (which + 1) * wide] = ref[:, pl.ds(start, wide)]
            low = len(taken) * wide
            out[:, low : low + wide] = ordered[:, pl.ds(start, wide)].astype(jnp.bfloat16)

    return local(
        kernel,
        [*arrays, stay, came],
        [(rows, (count + 1) * wide)] * len(steps) + [(rows, wide)] * len(early),
        [pltpu.VMEM((rows, columns), jnp.float32)],
    )


def attend(own, other, rows):
    chips = len(own)
    total = 2 * chips * rows
    part = chips // 2 * rows
    scaling = 1.0 / math.sqrt(HD)
    grade = scaling * math.log2(math.e)
    operands = [block for part in (own, other) for blocks in part for block in blocks]
    inputs = len(operands)

    def kernel(*refs):
        taken = iter(refs)
        own_refs, other_refs = (
            [[next(taken) for _ in blocks] for blocks in part] for part in (own, other)
        )
        outs = refs[inputs : inputs + chips]
        gathered, query_sum, key_sum, value_sum, hidden = refs[inputs + chips :]
        chip, core, _ = where_am_i()

        def piece(blocks, which, head):
            at = which * 3 + head
            if len(blocks) == 2 and which == 3:
                blocks, at = blocks[1:], head
            return blocks[0][:, pl.ds(pl.multiple_of(at * HD, HD), HD)].astype(jnp.float32)

        def spots(step):
            late = jnp.where((chip ^ step) >= chips // 2, 1, 0)
            start = late * (2 * part) + ((chip ^ step) - late * (chips // 2)) * rows
            return (
                pl.ds(pl.multiple_of(start, 8), rows),
                pl.ds(pl.multiple_of(start + part, 8), rows),
            )

        def place(shape, axis):
            at = lax.broadcasted_iota(jnp.int32, shape, axis).astype(jnp.float32)
            others = jnp.where(at < part, 0.0, 1.0)
            inside = at - others * part
            which = jnp.floor((inside + 0.5) * (1.0 / rows))
            side = jnp.abs(others - jnp.where(core == 1, 1.0, 0.0))
            return which * (2 * rows) + side * rows + (inside - which * rows)

        square = hidden.shape
        hidden[...] = jnp.where(place(square, 0) <= place(square, 1), 0.0, lowest)
        last, first, plain = ((((x,), (y,)), ((), ())) for x, y in ((1, 1), (0, 0), (1, 0)))
        for head in range(3):
            for which in range(4):
                for step in range(chips):
                    mine, others = spots(step)
                    gathered[which, mine, :] = piece(own_refs[step], which, head)
                    gathered[which, others, :] = piece(other_refs[step], which, head)
            query, keys, values, grads = (
                gathered[which].astype(jnp.bfloat16) for which in range(4)
            )
            for low in range(0, total, 2 * part):
                high = low + 2 * part
                q, g = query[low:high], grads[low:high]
                k, v = keys[:high], values[:high]
                scores = lax.dot_general(k, q, last, preferred_element_type=jnp.float32)
                below = scores[low:] + hidden[...]
                scores = jnp.concatenate([scores[:low], below]) if low else below
                expo = jnp.exp2((scores - jnp.max(scores, axis=0, keepdims=True)) * grade)
                products = lax.dot_general(v, g, last, preferred_element_type=jnp.float32)
                scale = 1.0 / jnp.sum(expo, axis=0, keepdims=True)
                delta = jnp.sum(expo * products, axis=0, keepdims=True) * scale
                weights = expo * scale
                score_grad = (weights * (products - delta)).astype(jnp.bfloat16)
                half = weights.astype(jnp.bfloat16)
                query_sum[low : low + part] = lax.dot_general(
                    score_grad[:, :part], k, first, preferred_element_type=jnp.float32
                )
                for start in range(0, high, 2 * part):
                    mine = slice(start, start + part)
                    for store, left, right in ((key_sum, score_grad, q), (value_sum, half, g)):
                        added = lax.dot_general(
                            left[mine], right, plain, preferred_element_type=jnp.float32
                        )
                        store[mine] = added if start == low else store[mine] + added
            for which, (store, factor) in enumerate(
                ((query_sum, scaling), (key_sum, scaling), (value_sum, 1.0))
            ):
                at = (which * 3 + head) * HD
                for step in range(chips):
                    outs[step][:, at : at + HD] = (store[spots(step)[0]] * factor).astype(jnp.bfloat16)

    big = pltpu.VMEM((total, HD), jnp.float32)
    return local(
        kernel,
        operands,
        [(rows, 9 * HD)] * chips,
        [
            pltpu.VMEM((4, total, HD), jnp.float32),
            big,
            big,
            big,
            pltpu.VMEM((2 * part, 2 * part), jnp.float32),
        ],
        10 * total * total * HD,
    )


def unpack(blocks, rows, columns):
    chips = len(blocks)
    wide = columns // chips

    def kernel(*refs):
        ins, outs = refs[:chips], refs[chips:]
        chip = where_am_i()[0]
        for step, ref in enumerate(ins):
            lanes = pl.ds(pl.multiple_of((chip ^ step) * wide, HD), wide)
            for which, out in enumerate(outs):
                out[:, lanes] = ref[:, which * wide : (which + 1) * wide]

    return local(kernel, blocks, [(rows, columns)] * 3, final=True)


def by_heads(query_rows, key_rows, value_rows, mid_grad, link_weight):
    rows, columns = query_rows.shape
    size = lax.axis_size("wide")
    chips = size // 2

    def cross(block, step):
        return held(lax.ppermute(block, "wide", [(i, i ^ step) for i in range(size)]))

    early, late = in_order(chips)
    own = {}
    arrays = [query_rows, key_rows, value_rows]
    ahead = pack(arrays, chips, early[:1], first=True)
    ahead += pack(arrays, chips, early[1:]) if early[1:] else []
    for step, block in zip(early, ahead):
        own[step] = [cross(block, 2 * step)]
    stay, leave = project(mid_grad, link_weight, 2)
    came = held(lax.ppermute(leave, "narrow", [(0, 1), (1, 0)]))
    rest = pack_grads(arrays, stay, came, chips, [0] + late, early)
    own[0] = [rest[0]]
    for step, block in zip(late, rest[1:]):
        own[step] = [cross(block, 2 * step)]
    for step, block in zip(early, rest[1 + len(late) :]):
        own[step].append(cross(block, 2 * step))
    own = [own[step] for step in range(chips)]
    other = [[cross(block, 1) for block in blocks] for blocks in own]
    done = attend(own, other, rows)
    own = [done[0]] + [cross(done[step], 2 * step) for step in range(1, chips)]
    return tuple(unpack(own, rows, columns))


def on_device(query_rows, key_rows, value_rows, mid_grad, link_weight):
    size = lax.axis_size("wide")
    rows, columns = query_rows.shape
    chips = size // 2
    fits = (
        size > 1
        and size & (size - 1) == 0
        and lax.axis_size("narrow") == 2
        and columns == chips * 3 * HD
        and chips > 1
        and (chips // 2 * rows) % 16 == 0
        and rows % 8 == 0
    )
    plan = by_heads if fits else by_rows
    return plan(query_rows, key_rows, value_rows, mid_grad, link_weight)


def by_rows(query_rows, key_rows, value_rows, mid_grad, link_weight):
    groups = lax.axis_size("narrow")
    patches = query_rows.shape[0]
    columns = query_rows.shape[1]
    heads_here = columns // HD
    scaling = 1.0 / math.sqrt(HD)
    local_patches = mid_grad.shape[0] // PATCH
    grouped = mid_grad.reshape(local_patches, groups, PATCH // groups, mid_grad.shape[1])
    moved = jnp.einsum(
        "abcm,pm->abcp",
        lax.all_to_all(grouped, "narrow", split_axis=1, concat_axis=0, tiled=True),
        link_weight,
        preferred_element_type=jnp.float32,
    ).astype(jnp.bfloat16)
    incoming = moved.reshape(patches, columns)
    incoming_heads = incoming.reshape(patches, heads_here, HD)
    query_heads = query_rows.reshape(patches, heads_here, HD)
    key_heads = key_rows.reshape(patches, heads_here, HD)
    value_heads = value_rows.reshape(patches, heads_here, HD)
    own_pos = lax.axis_index("wide") * patches + jnp.arange(patches, dtype=jnp.int32)
    total_rows = patches * lax.axis_size("wide")
    empty_store = jnp.zeros((total_rows, columns), jnp.bfloat16)
    fold_start = (
        jnp.full((heads_here, patches), lowest, jnp.float32),
        jnp.zeros((heads_here, patches), jnp.float32),
        jnp.zeros((heads_here, patches), jnp.float32),
        empty_store,
        empty_store,
    )
    pieces = (
        lax.all_gather(key_rows, "wide", axis=0, tiled=True),
        lax.all_gather(value_rows, "wide", axis=0, tiled=True),
    )
    key_piece, value_piece = pieces
    piece_rows = key_piece.shape[0]
    key_split = key_piece.reshape(piece_rows, heads_here, HD)
    value_split = value_piece.reshape(piece_rows, heads_here, HD)
    piece_pos = jnp.arange(piece_rows, dtype=jnp.int32)
    allowed = piece_pos[None, None, :] <= own_pos[None, :, None]
    scores = (
        jnp.einsum("qhd,khd->hqk", query_heads, key_split, preferred_element_type=jnp.float32)
        * scaling
    )
    scores = jnp.where(allowed, scores, lowest)
    products = jnp.einsum(
        "qhd,khd->hqk", incoming_heads, value_split, preferred_element_type=jnp.float32
    )
    old_max, _, _ = fold_start[:3]
    new_max = jnp.maximum(old_max, jnp.max(scores, axis=2))
    expo = jnp.where(allowed, jnp.exp(scores - new_max[:, :, None]), 0.0)
    stats = (new_max, jnp.sum(expo, axis=2), jnp.sum(expo * products, axis=2))
    key_store = pieces[0]
    value_store = pieces[1]
    folded = stats + (key_store, value_store)
    run_max, run_total, run_tilt = (folded[0], folded[1], folded[2])
    log_total = run_max + jnp.log(run_total)
    row_delta = run_tilt / run_total
    key_all = folded[3].reshape(total_rows, heads_here, HD)
    value_all = folded[4].reshape(total_rows, heads_here, HD)
    every_pos = jnp.arange(total_rows, dtype=jnp.int32)
    allowed_q = every_pos[None, None, :] <= own_pos[None, :, None]
    scores_q = (
        jnp.einsum("qhd,khd->hqk", query_heads, key_all, preferred_element_type=jnp.float32)
        * scaling
    )
    products_q = jnp.einsum(
        "qhd,khd->hqk", incoming_heads, value_all, preferred_element_type=jnp.float32
    )
    weights_q = jnp.where(
        allowed_q, jnp.exp(jnp.where(allowed_q, scores_q, lowest) - log_total[:, :, None]), 0.0
    )
    score_grad_q = (weights_q * (products_q - row_delta[:, :, None])).astype(jnp.bfloat16)
    query_accum = jnp.einsum(
        "hqk,khd->qhd", score_grad_q, key_all, preferred_element_type=jnp.float32
    )
    query_grad = (query_accum * scaling).astype(jnp.bfloat16).reshape(patches, columns)
    total_all, delta_all = (
        lax.all_gather(log_total, "wide", axis=1, tiled=True),
        lax.all_gather(row_delta, "wide", axis=1, tiled=True),
    )
    query_piece = lax.all_gather(query_rows, "wide", axis=0, tiled=True)
    grad_piece = lax.all_gather(incoming, "wide", axis=0, tiled=True)
    piece_rows = query_piece.shape[0]
    query_split = query_piece.reshape(piece_rows, heads_here, HD)
    grad_split = grad_piece.reshape(piece_rows, heads_here, HD)
    piece_pos = jnp.arange(piece_rows, dtype=jnp.int32)
    allowed = own_pos[None, None, :] <= piece_pos[None, :, None]
    scores = (
        jnp.einsum("qhd,khd->hqk", query_split, key_heads, preferred_element_type=jnp.float32)
        * scaling
    )
    scores = jnp.where(allowed, scores, lowest)
    products = jnp.einsum(
        "qhd,khd->hqk", grad_split, value_heads, preferred_element_type=jnp.float32
    )
    weights = jnp.where(allowed, jnp.exp(scores - total_all[:, :, None]), 0.0)
    score_grad = (weights * (products - delta_all[:, :, None])).astype(jnp.bfloat16)
    key_accum = jnp.einsum(
        "hqk,qhd->khd", score_grad, query_split, preferred_element_type=jnp.float32
    )
    value_accum = jnp.einsum(
        "hqk,qhd->khd", weights.astype(jnp.bfloat16), grad_split, preferred_element_type=jnp.float32
    )
    key_accum, value_accum = (key_accum, value_accum)
    key_grad = (key_accum * scaling).astype(jnp.bfloat16).reshape(patches, columns)
    value_grad = value_accum.astype(jnp.bfloat16).reshape(patches, columns)
    return (query_grad, key_grad, value_grad)


def solution(mesh):
    in_specs = (
        P("wide", "narrow"),
        P("wide", "narrow"),
        P("wide", "narrow"),
        P(("wide", "narrow"), None),
        P(),
    )
    out_specs = (P("wide", "narrow"), P("wide", "narrow"), P("wide", "narrow"))
    return jax.shard_map(
        on_device, mesh=mesh, in_specs=in_specs, out_specs=out_specs, check_vma=False
    )
```

```python
import math

import jax
import jax.numpy as jnp
from jax import lax
from jax.experimental import pallas as pl
from jax.experimental.pallas import tpu as pltpu
from jax.sharding import PartitionSpec as P


HD = 128
PATCH = 8
ROOM = 24 << 20


lowest = -1e30


def in_order(chips):
    far, near = far_and_near(chips)
    return far[:3], far[3:] + near


def far_and_near(chips):
    return list(range(chips // 2, chips)), list(range(1, chips // 2))[::-1]


def local(kernel, ins, shapes, scratch=(), flops=0, final=False, afar=()):
    vmem, anywhere = (pl.BlockSpec(memory_space=space) for space in (pltpu.VMEM, pltpu.HBM))
    outs = [
        jax.ShapeDtypeStruct(shape, jnp.bfloat16) if final else pltpu.VMEM(shape, jnp.bfloat16)
        for shape in shapes
    ]
    moved = 2 * (sum(array.size for array in ins) + sum(math.prod(shape) for shape in shapes))
    return pl.pallas_call(
        kernel,
        in_specs=[anywhere if i in afar else vmem for i in range(len(ins))],
        out_specs=[vmem] * len(shapes),
        out_shape=outs,
        scratch_shapes=list(scratch),
        compiler_params=pltpu.CompilerParams(vmem_limit_bytes=ROOM),
        cost_estimate=pl.CostEstimate(flops=flops, bytes_accessed=moved, transcendentals=0),
    )(*(pltpu.with_memory_space_constraint(x, pltpu.HBM) if i in afar else x for i, x in enumerate(ins)))


def held(array):
    return pltpu.with_memory_space_constraint(array, pltpu.VMEM)


def where_am_i():
    me = lax.axis_index("wide")
    return me // 2, me % 2, lax.axis_index("narrow")


def project(mid_grad, link_weight, groups):
    rows, depth = mid_grad.shape
    features = link_weight.shape[0]
    patches, each = rows // PATCH, PATCH // groups

    def kernel(grad_ref, link_ref, stay_ref, leave_ref, product):
        side = where_am_i()[2]
        for low in range(0, features, 256):
            result = lax.dot_general(
                grad_ref[...],
                link_ref[low : low + 256],
                (((1,), (1,)), ((), ())),
                preferred_element_type=jnp.float32,
            )
            for slab in range(result.shape[1] // HD):
                product[low // HD + slab] = result[:, slab * HD : (slab + 1) * HD]
        for out, group in ((stay_ref, side), (leave_ref, 1 - side)):
            for index in range(each):
                for slab in range(features // HD):
                    at = index * features + slab * HD
                    picked = product[slab, pl.ds(group * each + index, patches, stride=PATCH), :]
                    out[:, at : at + HD] = picked.astype(jnp.bfloat16)

    return local(
        kernel,
        [mid_grad, link_weight],
        [(patches, each * features)] * 2,
        [pltpu.VMEM((features // HD, rows, HD), jnp.float32)],
        2 * rows * depth * features,
    )


def pack(arrays, chips, steps, first=False):
    rows, columns = arrays[0].shape
    wide = columns // chips
    count = len(arrays)

    def kernel(*refs):
        ins, outs = refs[:count], refs[count : count + len(steps)]
        chip = where_am_i()[0]
        copies = []
        for at, (out, step) in enumerate(zip(outs, steps)):
            start = pl.multiple_of((chip ^ step) * wide, HD)
            for which, ref in enumerate(ins):
                source, target = ref.at[:, pl.ds(start, wide)], out.at[:, which * wide : (which + 1) * wide]
                if first:
                    arrived = refs[-1].at[at * count + which]
                    copies.append(pltpu.make_async_copy(source, target, arrived))
                    copies[-1].start()
                else:
                    target[...] = source[...]
        for copy in copies:
            copy.wait()

    return local(
        kernel,
        arrays,
        [(rows, count * wide)] * len(steps),
        [pltpu.SemaphoreType.DMA((count * len(steps),))] if first else (),
        flops=5 * 10**9 if first else 0,
        afar=range(count) if first else (),
    )


def pack_grads(arrays, stay, came, chips, steps, early):
    rows, columns = arrays[0].shape
    wide = columns // chips
    half = stay.shape[0]
    count = len(arrays)

    def kernel(*refs):
        ins, (stay_ref, came_ref) = refs[:count], refs[count : count + 2]
        outs, ordered = refs[count + 2 : -1], refs[-1]
        chip, _, side = where_am_i()
        mine, others = stay_ref[...].astype(jnp.float32), came_ref[...].astype(jnp.float32)
        ordered[:half] = jnp.where(side == 0, mine, others)
        ordered[half:] = jnp.where(side == 0, others, mine)
        for out, step in zip(outs, tuple(steps) + tuple(early)):
            start = pl.multiple_of((chip ^ step) * wide, HD)
            taken = ins if step in steps else ()
            for which, ref in enumerate(taken):
                out[:, which * wide : (which + 1) * wide] = ref[:, pl.ds(start, wide)]
            low = len(taken) * wide
            out[:, low : low + wide] = ordered[:, pl.ds(start, wide)].astype(jnp.bfloat16)

    return local(
        kernel,
        [*arrays, stay, came],
        [(rows, (count + 1) * wide)] * len(steps) + [(rows, wide)] * len(early),
        [pltpu.VMEM((rows, columns), jnp.float32)],
    )


def attend(own, other, rows):
    chips = len(own)
    total = 2 * chips * rows
    part = chips * rows
    scaling = 1.0 / math.sqrt(HD)
    grade = scaling * math.log2(math.e)
    operands = [block for part in (own, other) for blocks in part for block in blocks]
    inputs = len(operands)

    def kernel(*refs):
        taken = iter(refs)
        own_refs, other_refs = (
            [[next(taken) for _ in blocks] for blocks in part] for part in (own, other)
        )
        outs = refs[inputs : inputs + chips]
        gathered, query_sum, key_sum, value_sum, hidden = refs[inputs + chips :]
        chip, core, _ = where_am_i()

        def piece(blocks, which, head):
            at = which * 3 + head
            if len(blocks) == 2 and which == 3:
                blocks, at = blocks[1:], head
            return blocks[0][:, pl.ds(pl.multiple_of(at * HD, HD), HD)].astype(jnp.float32)

        def spots(step):
            start = (chip ^ step) * rows
            return (
                pl.ds(pl.multiple_of(start, 8), rows),
                pl.ds(pl.multiple_of(start + part, 8), rows),
            )

        def place(shape, axis):
            at = lax.broadcasted_iota(jnp.int32, shape, axis).astype(jnp.float32)
            others = jnp.where(at < part, 0.0, 1.0)
            inside = at - others * part
            which = jnp.floor((inside + 0.5) * (1.0 / rows))
            side = jnp.abs(others - jnp.where(core == 1, 1.0, 0.0))
            return which * (2 * rows) + side * rows + (inside - which * rows)

        hidden[...] = jnp.where(place((total, 1), 0) <= place((1, total), 1), 0.0, lowest)
        last, first, plain = ((((x,), (y,)), ((), ())) for x, y in ((1, 1), (0, 0), (1, 0)))
        for head in range(3):
            for which in range(4):
                for step in range(chips):
                    mine, others = spots(step)
                    gathered[which, mine, :] = piece(own_refs[step], which, head)
                    gathered[which, others, :] = piece(other_refs[step], which, head)
            query, keys, values, grads = (
                gathered[which].astype(jnp.bfloat16) for which in range(4)
            )
            scores = lax.dot_general(keys, query, last, preferred_element_type=jnp.float32)
            scores = scores + hidden[...]
            expo = jnp.exp2((scores - jnp.max(scores, axis=0, keepdims=True)) * grade)
            products = lax.dot_general(values, grads, last, preferred_element_type=jnp.float32)
            scale = 1.0 / jnp.sum(expo, axis=0, keepdims=True)
            delta = jnp.sum(expo * products, axis=0, keepdims=True) * scale
            weights = expo * scale
            score_grad = (weights * (products - delta)).astype(jnp.bfloat16)
            half = weights.astype(jnp.bfloat16)
            query_sum[...] = lax.dot_general(
                score_grad[:, :part], keys, first, preferred_element_type=jnp.float32
            )
            for store, left, right in ((key_sum, score_grad, query), (value_sum, half, grads)):
                store[...] = lax.dot_general(
                    left[:part], right, plain, preferred_element_type=jnp.float32
                )
            for which, (store, factor) in enumerate(
                ((query_sum, scaling), (key_sum, scaling), (value_sum, 1.0))
            ):
                at = (which * 3 + head) * HD
                for step in range(chips):
                    outs[step][:, at : at + HD] = (store[spots(step)[0]] * factor).astype(jnp.bfloat16)

    big = pltpu.VMEM((part, HD), jnp.float32)
    return local(
        kernel,
        operands,
        [(rows, 9 * HD)] * chips,
        [
            pltpu.VMEM((4, total, HD), jnp.float32),
            big,
            big,
            big,
            pltpu.VMEM((total, total), jnp.float32),
        ],
        10 * total * total * HD,
    )


def unpack(blocks, rows, columns):
    chips = len(blocks)
    wide = columns // chips

    def kernel(*refs):
        ins, outs = refs[:chips], refs[chips:]
        chip = where_am_i()[0]
        for step, ref in enumerate(ins):
            lanes = pl.ds(pl.multiple_of((chip ^ step) * wide, HD), wide)
            for which, out in enumerate(outs):
                out[:, lanes] = ref[:, which * wide : (which + 1) * wide]

    return local(kernel, blocks, [(rows, columns)] * 3, final=True)


def by_heads(query_rows, key_rows, value_rows, mid_grad, link_weight):
    rows, columns = query_rows.shape
    size = lax.axis_size("wide")
    chips = size // 2

    def cross(block, step):
        return held(lax.ppermute(block, "wide", [(i, i ^ step) for i in range(size)]))

    early, late = in_order(chips)
    own = {}
    arrays = [query_rows, key_rows, value_rows]
    ahead = pack(arrays, chips, early[:1], first=True)
    ahead += pack(arrays, chips, early[1:]) if early[1:] else []
    for step, block in zip(early, ahead):
        own[step] = [cross(block, 2 * step)]
    stay, leave = project(mid_grad, link_weight, 2)
    came = held(lax.ppermute(leave, "narrow", [(0, 1), (1, 0)]))
    rest = pack_grads(arrays, stay, came, chips, [0] + late, early)
    own[0] = [rest[0]]
    for step, block in zip(late, rest[1:]):
        own[step] = [cross(block, 2 * step)]
    for step, block in zip(early, rest[1 + len(late) :]):
        own[step].append(cross(block, 2 * step))
    own = [own[step] for step in range(chips)]
    other = [[cross(block, 1) for block in blocks] for blocks in own]
    done = attend(own, other, rows)
    own = [done[0]] + [cross(done[step], 2 * step) for step in range(1, chips)]
    return tuple(unpack(own, rows, columns))


def on_device(query_rows, key_rows, value_rows, mid_grad, link_weight):
    size = lax.axis_size("wide")
    rows, columns = query_rows.shape
    chips = size // 2
    fits = (
        size > 1
        and size & (size - 1) == 0
        and lax.axis_size("narrow") == 2
        and columns == chips * 3 * HD
        and chips > 1
        and (chips * rows) % 16 == 0
        and rows % 8 == 0
    )
    plan = by_heads if fits else by_rows
    return plan(query_rows, key_rows, value_rows, mid_grad, link_weight)


def by_rows(query_rows, key_rows, value_rows, mid_grad, link_weight):
    groups = lax.axis_size("narrow")
    patches = query_rows.shape[0]
    columns = query_rows.shape[1]
    heads_here = columns // HD
    scaling = 1.0 / math.sqrt(HD)
    local_patches = mid_grad.shape[0] // PATCH
    grouped = mid_grad.reshape(local_patches, groups, PATCH // groups, mid_grad.shape[1])
    moved = jnp.einsum(
        "abcm,pm->abcp",
        lax.all_to_all(grouped, "narrow", split_axis=1, concat_axis=0, tiled=True),
        link_weight,
        preferred_element_type=jnp.float32,
    ).astype(jnp.bfloat16)
    incoming = moved.reshape(patches, columns)
    incoming_heads = incoming.reshape(patches, heads_here, HD)
    query_heads = query_rows.reshape(patches, heads_here, HD)
    key_heads = key_rows.reshape(patches, heads_here, HD)
    value_heads = value_rows.reshape(patches, heads_here, HD)
    own_pos = lax.axis_index("wide") * patches + jnp.arange(patches, dtype=jnp.int32)
    total_rows = patches * lax.axis_size("wide")
    empty_store = jnp.zeros((total_rows, columns), jnp.bfloat16)
    fold_start = (
        jnp.full((heads_here, patches), lowest, jnp.float32),
        jnp.zeros((heads_here, patches), jnp.float32),
        jnp.zeros((heads_here, patches), jnp.float32),
        empty_store,
        empty_store,
    )
    pieces = (
        lax.all_gather(key_rows, "wide", axis=0, tiled=True),
        lax.all_gather(value_rows, "wide", axis=0, tiled=True),
    )
    key_piece, value_piece = pieces
    piece_rows = key_piece.shape[0]
    key_split = key_piece.reshape(piece_rows, heads_here, HD)
    value_split = value_piece.reshape(piece_rows, heads_here, HD)
    piece_pos = jnp.arange(piece_rows, dtype=jnp.int32)
    allowed = piece_pos[None, None, :] <= own_pos[None, :, None]
    scores = (
        jnp.einsum("qhd,khd->hqk", query_heads, key_split, preferred_element_type=jnp.float32)
        * scaling
    )
    scores = jnp.where(allowed, scores, lowest)
    products = jnp.einsum(
        "qhd,khd->hqk", incoming_heads, value_split, preferred_element_type=jnp.float32
    )
    old_max, _, _ = fold_start[:3]
    new_max = jnp.maximum(old_max, jnp.max(scores, axis=2))
    expo = jnp.where(allowed, jnp.exp(scores - new_max[:, :, None]), 0.0)
    stats = (new_max, jnp.sum(expo, axis=2), jnp.sum(expo * products, axis=2))
    key_store = pieces[0]
    value_store = pieces[1]
    folded = stats + (key_store, value_store)
    run_max, run_total, run_tilt = (folded[0], folded[1], folded[2])
    log_total = run_max + jnp.log(run_total)
    row_delta = run_tilt / run_total
    key_all = folded[3].reshape(total_rows, heads_here, HD)
    value_all = folded[4].reshape(total_rows, heads_here, HD)
    every_pos = jnp.arange(total_rows, dtype=jnp.int32)
    allowed_q = every_pos[None, None, :] <= own_pos[None, :, None]
    scores_q = (
        jnp.einsum("qhd,khd->hqk", query_heads, key_all, preferred_element_type=jnp.float32)
        * scaling
    )
    products_q = jnp.einsum(
        "qhd,khd->hqk", incoming_heads, value_all, preferred_element_type=jnp.float32
    )
    weights_q = jnp.where(
        allowed_q, jnp.exp(jnp.where(allowed_q, scores_q, lowest) - log_total[:, :, None]), 0.0
    )
    score_grad_q = (weights_q * (products_q - row_delta[:, :, None])).astype(jnp.bfloat16)
    query_accum = jnp.einsum(
        "hqk,khd->qhd", score_grad_q, key_all, preferred_element_type=jnp.float32
    )
    query_grad = (query_accum * scaling).astype(jnp.bfloat16).reshape(patches, columns)
    total_all, delta_all = (
        lax.all_gather(log_total, "wide", axis=1, tiled=True),
        lax.all_gather(row_delta, "wide", axis=1, tiled=True),
    )
    query_piece = lax.all_gather(query_rows, "wide", axis=0, tiled=True)
    grad_piece = lax.all_gather(incoming, "wide", axis=0, tiled=True)
    piece_rows = query_piece.shape[0]
    query_split = query_piece.reshape(piece_rows, heads_here, HD)
    grad_split = grad_piece.reshape(piece_rows, heads_here, HD)
    piece_pos = jnp.arange(piece_rows, dtype=jnp.int32)
    allowed = own_pos[None, None, :] <= piece_pos[None, :, None]
    scores = (
        jnp.einsum("qhd,khd->hqk", query_split, key_heads, preferred_element_type=jnp.float32)
        * scaling
    )
    scores = jnp.where(allowed, scores, lowest)
    products = jnp.einsum(
        "qhd,khd->hqk", grad_split, value_heads, preferred_element_type=jnp.float32
    )
    weights = jnp.where(allowed, jnp.exp(scores - total_all[:, :, None]), 0.0)
    score_grad = (weights * (products - delta_all[:, :, None])).astype(jnp.bfloat16)
    key_accum = jnp.einsum(
        "hqk,qhd->khd", score_grad, query_split, preferred_element_type=jnp.float32
    )
    value_accum = jnp.einsum(
        "hqk,qhd->khd", weights.astype(jnp.bfloat16), grad_split, preferred_element_type=jnp.float32
    )
    key_accum, value_accum = (key_accum, value_accum)
    key_grad = (key_accum * scaling).astype(jnp.bfloat16).reshape(patches, columns)
    value_grad = value_accum.astype(jnp.bfloat16).reshape(patches, columns)
    return (query_grad, key_grad, value_grad)


def solution(mesh):
    in_specs = (
        P("wide", "narrow"),
        P("wide", "narrow"),
        P("wide", "narrow"),
        P(("wide", "narrow"), None),
        P(),
    )
    out_specs = (P("wide", "narrow"), P("wide", "narrow"), P("wide", "narrow"))
    return jax.shard_map(
        on_device, mesh=mesh, in_specs=in_specs, out_specs=out_specs, check_vma=False
    )
```
